256 devices in a mesh: tm: 8 (over y, core), doc: 32 (over x, z).
Axes of the slice: x: 4, y: 4, z: 8, core: 2. Of those that a mesh axis runs over, the one named last changes fastest.
Arguments:
- beta_mean: float32 [16, 65536, 200], P('tm', 'doc'), may hold values from -9 to 230
- word_ids: int32 [8192, 128], P(('tm', 'doc')), may hold values from 0 to 65535, as said below
- word_counts: int32 [8192, 128], P(('tm', 'doc')), may hold values from 0 to 8
- doc_slice: int32 [8192], P(('tm', 'doc')), may hold values from 0 to 15, as said below
- dirichlet: float32 [200], replicated, may hold values from 0.05 to 0.5
- drift_var: float32 [200], replicated, may hold values from 0.002 to 0.5
- obs_var: float32 [200], replicated, may hold values from 0.05 to 1
Outputs:
- smoothed_mean: float32 [16, 65536, 200], P('tm', 'doc')
- doc_topics: float32 [8192, 200], P(('tm', 'doc'))
The draws below stay inside these ranges and needn't reach their ends.
Inputs may be any that keep to these rules, and one draw needn't show every extreme that they name: `word_ids`: vocabulary range b holds the words b * 2048 to (b + 1) * 2048 - 1. Over the 4096 slots of each aligned block of 32 documents, at most 160 hold words of one range; in every block some range holds exactly 160, the same range for all blocks of the same 1024 documents. A word may fill several slots of a document. `doc_slice`: the documents of rows i * 1024 to (i + 1) * 1024 - 1 belong to slices i * 2 to (i + 1) * 2 - 1.
All inputs are finite; a program needn't handle non-finite values.
Results may differ from the reference program's by a relative error of at most 0.0034.
Values may be sent and summed in bfloat16 or wider, within the bound.
No kernel may reach another device: no remote copies, remote signals or barrier semaphores. Data moves between devices by JAX's collectives and lax.ppermute only.
A program may use at most 128 MiB of HBM per device.

```python
import math
import jax
import jax.numpy as jnp
from jax import lax

TOPICS = 200
VOCAB = 65536
TOKW = 128
E_ITERS = 4
SLICE_DEV = 2
DOC_DEV = 32
SLICES = 16
DOCS = 8192
CAP = 160
N_TM = 8
N_DOC = 32


def draw_beta_mean(key, part):
    shape = (SLICES, VOCAB, TOPICS)
    first_key = jax.random.fold_in(key, 0)
    return jnp.clip(jax.random.normal(first_key, shape, jnp.float32) * 1.5, -9.0, 9.0)


def draw_word_ids(key, part):
    block_total = N_TM * N_DOC
    slot_total = DOC_DEV * TOKW
    room = N_DOC * CAP
    range_width = VOCAB // N_DOC
    keys = jax.random.split(key, 4)
    full_range = jax.random.randint(keys[0], (N_TM,), 0, N_DOC)
    full_block = jnp.repeat(full_range, N_DOC)[:, None]
    room_index = jnp.arange(room, dtype=jnp.int32)[None, :]
    room_owner = room_index // CAP
    scores = jax.random.randint(keys[1], (block_total, room), 0, 4096) + (N_DOC - 1 - room_owner) * (2048 // N_DOC)
    ranked = jnp.where(room_owner == full_block, room_index - room, scores * room + room_index)
    chosen = jnp.argsort(ranked, axis=1)[:, :slot_total]
    owners = (chosen // CAP).astype(jnp.int32)
    owners = jax.random.permutation(keys[2], owners, axis=1, independent=True)
    local_word = jax.random.randint(keys[3], (block_total, slot_total), 0, range_width)
    return (owners * range_width + local_word).reshape(DOCS, TOKW).astype(jnp.int32)


def draw_doc_slice(key, part):
    groups = jnp.arange(DOCS, dtype=jnp.int32) // (DOC_DEV * N_DOC)
    return (groups * SLICE_DEV + jax.random.randint(key, (DOCS,), 0, SLICE_DEV)).astype(jnp.int32)


def with_ends(array, rng, low, high):
    longest = array.shape.index(max(array.shape))
    spots = []
    for shift in (0, 1):
        where = [jax.random.randint(jax.random.fold_in(rng, axis), (), 0, length) for axis, length in enumerate(array.shape)]
        where[longest] = (where[longest] + shift) % array.shape[longest]
        spots.append(tuple(where))
    return array.at[spots[0]].set(low).at[spots[1]].set(high)


def setup_inputs(seed: int = 0) -> dict:
    streams_of = jax.random.split(jax.random.key(seed), 8)
    return {
        "beta_mean": draw_beta_mean(jax.random.fold_in(streams_of[7], 71), 0),
        "word_ids": draw_word_ids(jax.random.fold_in(streams_of[7], 71), 0),
        "word_counts": with_ends(jax.random.randint(streams_of[2], (DOCS, TOKW), 0, 9), jax.random.fold_in(streams_of[2], 1), 0, 8).astype(jnp.int32),
        "doc_slice": draw_doc_slice(jax.random.fold_in(streams_of[7], 71), 0),
        "dirichlet": jnp.clip(jnp.exp(jax.random.uniform(streams_of[4], (TOPICS,), jnp.float32, math.log(0.05), math.log(0.5))), 0.05, 0.5),
        "drift_var": jnp.clip(jnp.exp(jax.random.uniform(streams_of[5], (TOPICS,), jnp.float32, math.log(0.002), math.log(0.5))), 0.002, 0.5),
        "obs_var": jnp.clip(jnp.exp(jax.random.uniform(streams_of[6], (TOPICS,), jnp.float32, math.log(0.05), math.log(1.0))), 0.05, 1.0),
    }


pseudo_count = 0.1
prior_var = 1.0


def digamma_series(value):
    correction = jnp.zeros_like(value)
    for shift_step in range(6):
        correction = correction + 1.0 / (value + float(shift_step))
    shifted = value + 6.0
    inverse = 1.0 / shifted
    inverse_square = inverse * inverse
    series = inverse_square * (1.0 / 12.0 - inverse_square * (1.0 / 120.0 - inverse_square * (1.0 / 252.0)))
    return jnp.log(shifted) - 0.5 * inverse - series - correction


def expectation(tok_beta, tok_count, dirichlet):
    doc_gamma = dirichlet[None, :] + jnp.sum(tok_count, axis=1, keepdims=True) / dirichlet.shape[0]
    for iteration in range(E_ITERS):
        log_theta = digamma_series(doc_gamma) - digamma_series(jnp.sum(doc_gamma, axis=1, keepdims=True))
        theta_exp = jnp.exp(log_theta)
        norm_tok = jnp.einsum("dk,dnk->dn", theta_exp, tok_beta, precision=lax.Precision.HIGHEST, preferred_element_type=jnp.float32)
        slot_ratio = tok_count / norm_tok
        doc_gamma = dirichlet[None, :] + theta_exp * jnp.einsum("dn,dnk->dk", slot_ratio, tok_beta, precision=lax.Precision.HIGHEST, preferred_element_type=jnp.float32)
    return doc_gamma, theta_exp, slot_ratio


def variances(drift_var, obs_var, length):
    def advance(filt_prev, placeholder):
        predicted = filt_prev + drift_var
        gain_now = predicted / (predicted + obs_var)
        filt_now = (1.0 - gain_now) * predicted
        return filt_now, (gain_now, filt_now)

    initial = jnp.full(drift_var.shape, prior_var, jnp.float32)
    final_var, outputs = lax.scan(advance, initial, None, length=length)
    return outputs


def reference(beta_mean, word_ids, word_counts, doc_slice, dirichlet, drift_var, obs_var):
    vocab_top = jnp.max(beta_mean, axis=1, keepdims=True)
    log_norm = vocab_top + jnp.log(jnp.sum(jnp.exp(beta_mean - vocab_top), axis=1, keepdims=True))
    expected_beta = jnp.exp(beta_mean - log_norm).astype(jnp.bfloat16).reshape(SLICES * VOCAB, TOPICS)
    block_count = DOCS // DOC_DEV
    slot_rows = (doc_slice[:, None] * VOCAB + word_ids).astype(jnp.int32).reshape(block_count, DOC_DEV, TOKW)
    counts_all = word_counts.astype(jnp.float32).reshape(block_count, DOC_DEV, TOKW)

    def one_block(block_index, running):
        word_stats, gamma_all = running
        rows_here = lax.dynamic_index_in_dim(slot_rows, block_index, 0, keepdims=False)
        tok_count = lax.dynamic_index_in_dim(counts_all, block_index, 0, keepdims=False)
        tok_beta = expected_beta[rows_here].astype(jnp.float32)
        doc_gamma, theta_exp, slot_ratio = expectation(tok_beta, tok_count, dirichlet)
        slot_terms = theta_exp[:, None, :] * slot_ratio[:, :, None] * tok_beta
        word_stats = word_stats.at[rows_here.reshape(-1)].add(slot_terms.reshape(-1, TOPICS))
        gamma_all = lax.dynamic_update_slice_in_dim(gamma_all, doc_gamma, block_index * DOC_DEV, 0)
        return word_stats, gamma_all

    initial = (jnp.zeros((SLICES * VOCAB, TOPICS), jnp.float32), jnp.zeros((DOCS, TOPICS), jnp.float32))
    word_stats, gamma_all = lax.fori_loop(0, block_count, one_block, initial)
    word_stats = word_stats.reshape(SLICES, VOCAB, TOPICS)
    gains, filt_var = variances(drift_var, obs_var, SLICES)

    def forward_step(mean_prev, inputs):
        gain_now, stats_now = inputs
        pseudo_now = jnp.log(stats_now + pseudo_count)
        mean_now = (1.0 - gain_now)[None, :] * mean_prev + gain_now[None, :] * pseudo_now
        return mean_now, mean_now

    last_mean, filtered = lax.scan(forward_step, jnp.zeros((VOCAB, TOPICS), jnp.float32), (gains, word_stats))
    smooth_gain = filt_var / (filt_var + drift_var[None, :])
    smooth_gain = smooth_gain.at[SLICES - 1].set(0.0)

    def backward_step(next_mean, inputs):
        weight, filt_now = inputs
        smooth_now = (1.0 - weight)[None, :] * filt_now + weight[None, :] * next_mean
        return smooth_now, smooth_now

    last_smooth, smoothed = lax.scan(backward_step, jnp.zeros((VOCAB, TOPICS), jnp.float32), (smooth_gain, filtered), reverse=True)
    return smoothed, gamma_all
```

```python
import functools
import math

import jax
import jax.numpy as jnp
from jax import lax
from jax.experimental import pallas as pl
from jax.experimental.pallas import tpu as pltpu
from jax.sharding import PartitionSpec as P

E_ITERS = 4
PSEUDO = 0.1
PRIOR_VAR = 1.0
LOG_PSEUDO = math.log(PSEUDO)
F32, BF16, I32 = jnp.float32, jnp.bfloat16, jnp.int32
NT = (((1,), (1,)), ((), ()))
TN = (((0,), (0,)), ((), ()))
SMEM = pl.BlockSpec(memory_space=pltpu.SMEM)


def iota(shape, axis):
    return lax.broadcasted_iota(I32, shape, axis)


def mm(a, b):
    return jnp.dot(a, b, preferred_element_type=F32)


def mmg(a, b, dims):
    return lax.dot_general(a, b, dims, preferred_element_type=F32)


def call(kernel, out_shape, *args, specs=None, scratch=()):
    specs = specs or [pl.BlockSpec()] * len(args)
    return pl.pallas_call(kernel, out_shape=out_shape, in_specs=specs, scratch_shapes=scratch)(*args)


def shape(dims, dtype):
    return jax.ShapeDtypeStruct(dims, dtype)


def place_kernel(peers, capacity, shift, ids_ref, counts_ref, slice_ref, code_ref, doc_ref, count_ref):
    docs, width = ids_ref.shape
    ids = ids_ref[...]
    owner = lax.shift_right_logical(ids, shift)
    word = ids & ((1 << shift) - 1)
    low = (word & 255).astype(F32)
    high = (lax.shift_right_logical(word, 8) + (slice_ref[...] << (shift - 8)) + 1).astype(F32)
    counts = counts_ref[...].astype(F32)
    before = (iota((width, width), 0) < iota((width, width), 1)).astype(F32).astype(BF16)
    owners = iota((peers, width), 0)
    ranks = iota((capacity, width), 0).astype(F32)
    hot = [(owners == owner[d : d + 1, :]).astype(F32) for d in range(docs)]
    inside = mm(jnp.concatenate(hot, axis=0).astype(BF16), before)
    start = jnp.zeros((peers, 1), F32)
    left, right = [], []
    for d in range(docs):
        mine = hot[d]
        rank = jnp.sum(mine * (inside[d * peers : (d + 1) * peers] + start), axis=0, keepdims=True)
        start = start + jnp.sum(mine, axis=1, keepdims=True)
        right.append((ranks == rank).astype(F32).astype(BF16))
        left.append(
            jnp.concatenate(
                [
                    mine * low[d : d + 1],
                    mine * high[d : d + 1],
                    mine * float(d),
                    mine * counts[d : d + 1],
                ],
                axis=0,
            ).astype(BF16)
        )
    placed = mmg(jnp.concatenate(left, axis=1), jnp.concatenate(right, axis=1), NT)
    low_p, high_p, doc_p, count_p = (placed[i * peers : (i + 1) * peers] for i in range(4))
    code_ref[...] = doc_p * 8192.0 + high_p * 256.0 + low_p
    doc_ref[...] = jnp.where(high_p > 0.5, doc_p, -1.0)
    count_ref[...] = count_p


def row_of(code, shift):
    at = (code & 8191) - 256
    return at & ((1 << shift) - 1), lax.shift_right_logical(at, shift) & 1


def fetch_kernel(shift, beta_ref, norm_ref, code_ref, table_ref, out_ref):
    rows, words = beta_ref.shape
    topics = rows // 2
    step = 16

    def fill(i, carry):
        at = pl.ds(pl.multiple_of(i * step, step), step)
        table_ref[at, :] = jnp.exp(beta_ref[at, :] - norm_ref[at, :]).astype(BF16)
        return carry

    lax.fori_loop(0, rows // step, fill, 0)
    chunk = code_ref.shape[1]

    def one(i, carry):
        word, part = row_of(code_ref[pl.ds(i, 1), :].astype(I32), shift)
        hot = (iota((words, chunk), 0) == word).astype(F32).astype(BF16)
        both = mm(table_ref[...], hot)
        picked = jnp.where(part == 0, both[:topics], both[topics:])
        out_ref[pl.ds(pl.multiple_of(i * chunk, chunk), chunk), :] = jnp.transpose(picked).astype(BF16)
        return carry

    lax.fori_loop(0, code_ref.shape[0], one, 0)


def digamma(value):
    correction = jnp.zeros_like(value)
    for j in range(6):
        correction = correction + 1.0 / (value + float(j))
    shifted = value + 6.0
    inverse = 1.0 / shifted
    square = inverse * inverse
    series = square * (1.0 / 12.0 - square * (1.0 / 120.0 - square * (1.0 / 252.0)))
    return jnp.log(shifted) - 0.5 * inverse - series - correction


def split(value):
    high = value.astype(BF16)
    return high, (value - high.astype(F32)).astype(BF16)


def estep_kernel(tok_ref, doc_ref, count_ref, counts_ref, dirichlet_ref, gamma_ref, theta_ref, ratio_ref):
    docs = counts_ref.shape[0]
    topics = dirichlet_ref.shape[1]
    places = tok_ref.shape[0]
    dirichlet = dirichlet_ref[...]
    total = jnp.sum(counts_ref[...].astype(F32), axis=1, keepdims=True)
    gamma = dirichlet + total / float(topics)
    doc = doc_ref[...]
    mask = iota((docs, places), 0) == doc.astype(I32)
    for step in range(E_ITERS):
        theta = jnp.exp(digamma(gamma) - digamma(jnp.sum(gamma, axis=1, keepdims=True)))
        norm = mmg(jnp.concatenate(split(theta), axis=0), tok_ref[...], NT)
        norm = norm[:docs] + norm[docs:]
        norm = jnp.sum(jnp.where(mask, norm, 0.0), axis=0, keepdims=True)
        ratio = jnp.where(doc >= 0.0, count_ref[...] / norm, 0.0)
        high, low = split(ratio)
        spread = jnp.concatenate(
            [jnp.where(mask, high.astype(F32), 0.0), jnp.where(mask, low.astype(F32), 0.0)], axis=0
        ).astype(BF16)
        part = mm(spread, tok_ref[...])
        gamma = dirichlet + theta * (part[:docs] + part[docs:])
    gamma_ref[...] = gamma
    theta_ref[...] = theta.astype(BF16)
    ratio_ref[0:1, :] = high.astype(F32)
    ratio_ref[1:2, :] = low.astype(F32)


def stats_kernel(
    shift, per, docs, core_ref, theta_ref, code_ref, high_ref, low_ref, table_ref, keep_ref, send_ref, total_ref
):
    groups, places = code_ref.shape
    rows, words = table_ref.shape
    topics = rows // 2
    sources = theta_ref.shape[0] // groups
    capacity = places // sources
    lane = iota((1, places), 1)
    offset = jnp.zeros((1, places), I32)
    for s in range(1, sources):
        offset = offset + jnp.where(lane >= s * capacity, docs, 0)
    for g in range(groups):
        code = code_ref[g : g + 1, :].astype(I32)
        word, part = row_of(code, shift)
        key = lax.shift_right_logical(code, 13) + offset
        theta = theta_ref[g * sources : (g + 1) * sources, :docs, :].reshape(sources * docs, topics)
        mask = iota((sources * docs, places), 0) == key
        high = jnp.where(mask, high_ref[g : g + 1, :], 0.0).astype(BF16)
        low = jnp.where(mask, low_ref[g : g + 1, :], 0.0).astype(BF16)
        factor = mmg(theta, high, TN) + mmg(theta, low, TN)
        factor = jnp.concatenate(
            [jnp.where(part == 0, factor, 0.0), jnp.where(part == 1, factor, 0.0)], axis=0
        ).astype(BF16)
        column = jnp.transpose(jnp.broadcast_to(word.astype(F32), (8, places)))[:, 0:1].astype(I32)

        def one(j, carry):
            at = pl.ds(pl.multiple_of(j * per, per), per)
            hot = (iota((places, per), 1) + j * per == column).astype(F32).astype(BF16)
            new = mm(factor, hot)
            if g == 0:
                total_ref[:, at] = new
            else:
                total_ref[:, at] = total_ref[:, at] + new
            return carry

        lax.fori_loop(0, words // per, one, 0)
    half = words // 2
    first = core_ref[0] == 0
    step = 16

    def finish(i, carry):
        at = pl.ds(pl.multiple_of(i * step, step), step)
        shifted = jnp.log(1.0 + (1.0 / PSEUDO) * (table_ref[at, :].astype(F32) * total_ref[at, :]))
        left, right = shifted[:, :half], shifted[:, half:]
        keep_ref[at, :] = jnp.where(first, left, right)
        send_ref[at, :] = jnp.where(first, right, left)
        return carry

    lax.fori_loop(0, rows // step, finish, 0)


G0, S0, H0, B0, PHI0, QK, KNEXT, PHI, WF0, WQ0, NCOEF = 0, 4, 8, 12, 16, 20, 21, 22, 23, 27, 32


def coef_kernel(chips, chip_ref, drift_ref, obs_ref, out_ref):
    per = 4
    length = chips * per
    drift, obs = drift_ref[...], obs_ref[...]
    one, zero = jnp.ones_like(drift), jnp.zeros_like(drift)
    var = one * PRIOR_VAR
    gain, smooth = [], []
    for t in range(length):
        pred = var + drift
        now = pred / (pred + obs)
        var = (1.0 - now) * pred
        gain.append(now)
        smooth.append(var / (var + drift) if t < length - 1 else zero)
    level, forward = zero, []
    for t in range(length):
        level = (1.0 - gain[t]) * level + gain[t]
        forward.append(level)
    ones_smoothed = [None] * length
    level = zero
    for t in reversed(range(length)):
        level = (1.0 - smooth[t]) * forward[t] + smooth[t] * level
        ones_smoothed[t] = level
    beta, phi, sigma, kappa = [], [], [], []
    for c in range(chips):
        run, back, k = one, one, zero
        for t in range(c * per, (c + 1) * per):
            run = run * (1.0 - gain[t])
            phi.append(run)
            beta.append(back * (1.0 - smooth[t]))
            k = k + beta[t] * run
            back = back * smooth[t]
        sigma.append(back)
        kappa.append(k)
    total = [phi[c * per + per - 1] for c in range(chips)]
    lead = [zero] * (chips + 1)
    for c in reversed(range(chips)):
        lead[c] = kappa[c] + sigma[c] * lead[c + 1] * total[c]
    chip = chip_ref[0]
    for c in range(chips):
        rows = [None] * NCOEF
        for u in range(per):
            t = c * per + u
            rows[G0 + u], rows[S0 + u], rows[H0 + u] = gain[t], smooth[t], ones_smoothed[t] * LOG_PSEUDO
            rows[B0 + u], rows[PHI0 + u] = beta[t], phi[t]
        rows[QK], rows[KNEXT], rows[PHI] = sigma[c] * lead[c + 1], lead[c + 1], total[c]
        for j in range(chips):
            behind, ahead = zero, zero
            if j < c:
                behind = one
                for m in range(j + 1, c):
                    behind = behind * total[m]
            if j > c:
                ahead = one
                for m in range(c + 1, j):
                    ahead = ahead * sigma[m]
            rows[WF0 + j], rows[WQ0 + j] = behind, ahead

        @pl.when(chip == c)
        def _():
            for r in range(NCOEF):
                out_ref[r : r + 1, :] = zero if rows[r] is None else rows[r]


def local_filter(coef, values):
    out, level = [], None
    for u in range(4):
        gain = coef[:, G0 + u : G0 + u + 1]
        level = gain * values[u] if level is None else (1.0 - gain) * level + gain * values[u]
        out.append(level)
    return out


def four(first, keep_ref, recv_ref, topics, at):
    own = [keep_ref[pl.ds(u * topics + at, 8), :] for u in range(2)]
    other = [recv_ref[pl.ds(u * topics + at, 8), :] for u in range(2)]
    return [jnp.where(first, own[u], other[u]) for u in range(2)] + [
        jnp.where(first, other[u], own[u]) for u in range(2)
    ]


def combine_kernel(where_ref, coef_ref, keep_ref, recv_ref, out_ref):
    chips, topics, _ = out_ref.shape
    first, chip = where_ref[1] == 0, where_ref[0]

    def block(i, carry):
        at = pl.multiple_of(i * 8, 8)
        coef = coef_ref[pl.ds(at, 8), :]
        local = local_filter(coef, four(first, keep_ref, recv_ref, topics, at))
        back = coef[:, QK : QK + 1] * local[3]
        for u in range(4):
            back = back + coef[:, B0 + u : B0 + u + 1] * local[u]
        for j in range(chips):
            out_ref[j, pl.ds(at, 8), :] = jnp.where(j > chip, local[3], back).astype(BF16)
        return carry

    lax.fori_loop(0, topics // 8, block, 0)


def smooth_kernel(where_ref, coef_ref, keep_ref, recv_ref, far_ref, own_ref, other_ref):
    chips, topics, _ = far_ref.shape
    first = where_ref[1] == 0

    def block(i, carry):
        at = pl.multiple_of(i * 8, 8)
        coef = coef_ref[pl.ds(at, 8), :]

        def take(r):
            return coef[:, r : r + 1]

        local = local_filter(coef, four(first, keep_ref, recv_ref, topics, at))
        entering = jnp.zeros_like(local[0])
        ahead = jnp.zeros_like(local[0])
        for j in range(chips):
            far = far_ref[j, pl.ds(at, 8), :].astype(F32)
            entering = entering + take(WF0 + j) * far
            ahead = ahead + take(WQ0 + j) * far
        level = ahead + take(KNEXT) * (local[3] + take(PHI) * entering)
        means = [None] * 4
        for u in reversed(range(4)):
            weight = take(S0 + u)
            level = (1.0 - weight) * (local[u] + take(PHI0 + u) * entering) + weight * level
            means[u] = level + take(H0 + u)
        for u in range(2):
            own_ref[u, pl.ds(at, 8), :] = jnp.where(first, means[u], means[u + 2])
            other_ref[u, pl.ds(at, 8), :] = jnp.where(first, means[u + 2], means[u])
        return carry

    lax.fori_loop(0, topics // 8, block, 0)


def per_device(beta_mean, word_ids, word_counts, doc_slice, dirichlet, drift_var, obs_var):
    slice_dev, vocab_shard, topics = beta_mean.shape
    docs, width = word_ids.shape
    peers = lax.axis_size("doc")
    time_peers = lax.axis_size("tm")
    here = lax.axis_index("tm")
    chip, core = here // 2, here % 2
    chips = time_peers // 2
    shift = vocab_shard.bit_length() - 1
    slots = docs * width
    capacity = slots * 5 // (4 * peers)
    places = peers * capacity
    half = vocab_shard // 2
    where = jnp.stack([chip, core]).astype(I32)

    beta = jnp.swapaxes(beta_mean, 1, 2)
    local_slice = (doc_slice - here * slice_dev).astype(I32).reshape(docs, 1)
    code, doc, count = call(
        functools.partial(place_kernel, peers, capacity, shift),
        [shape((peers, capacity), F32)] * 3,
        word_ids,
        word_counts,
        local_slice,
    )
    top = jnp.max(beta, axis=2)
    mass = jnp.sum(jnp.exp(beta - top[:, :, None]), axis=2)
    stats = jnp.concatenate([top.reshape(1, 1, -1), mass.reshape(1, 1, -1)], axis=2)
    outgoing = jnp.concatenate(
        [code.reshape(peers, 1, capacity), jnp.broadcast_to(stats, (peers, 1, stats.shape[2]))], axis=2
    )
    arrived = lax.all_to_all(outgoing, "doc", split_axis=0, concat_axis=0, tiled=True)
    coef = call(
        functools.partial(coef_kernel, chips),
        shape((NCOEF, topics), F32),
        where,
        drift_var.reshape(1, topics),
        obs_var.reshape(1, topics),
        specs=[SMEM, pl.BlockSpec(), pl.BlockSpec()],
    )
    coef = coef.T
    asked = arrived[:, 0, :capacity]
    tops = arrived[:, 0, capacity : capacity + slice_dev * topics]
    masses = arrived[:, 0, capacity + slice_dev * topics :]
    highest = jnp.max(tops, axis=0)
    log_norm = highest + jnp.log(jnp.sum(masses * jnp.exp(tops - highest), axis=0))
    chunk = 256
    table, fetched = call(
        functools.partial(fetch_kernel, shift),
        [shape((slice_dev * topics, vocab_shard), BF16), shape((places, topics), BF16)],
        beta.reshape(slice_dev * topics, vocab_shard),
        log_norm.reshape(-1, 1),
        asked.reshape(places // chunk, chunk),
    )
    replies = lax.all_to_all(
        fetched.reshape(peers, capacity, topics), "doc", split_axis=0, concat_axis=0, tiled=True
    )
    gamma, theta, ratio = call(
        estep_kernel,
        [shape((docs, topics), F32), shape((docs, topics), BF16), shape((2, places), F32)],
        replies.reshape(places, topics),
        doc.reshape(1, places),
        count.reshape(1, places),
        word_counts,
        dirichlet.reshape(1, topics),
    )
    ratio = jnp.swapaxes(ratio.reshape(2, peers, capacity), 0, 1).reshape(peers, 2 * capacity).astype(BF16)
    ratio = jnp.pad(ratio, ((0, 0), (0, 2 * topics - 2 * capacity))).reshape(peers, 2, topics)
    factors = jnp.concatenate([jnp.broadcast_to(theta[None], (peers, docs, topics)), ratio], axis=1)
    factors = lax.all_to_all(factors, "doc", split_axis=0, concat_axis=0, tiled=True)
    group = 4
    ratios = factors[:, docs:, :].reshape(peers, 2 * topics).astype(F32)
    keep, send = call(
        functools.partial(stats_kernel, shift, 256, docs),
        [shape((slice_dev * topics, half), F32)] * 2,
        core.astype(I32).reshape(1),
        factors,
        asked.reshape(group, places // group),
        ratios[:, :capacity].reshape(group, places // group),
        ratios[:, capacity : 2 * capacity].reshape(group, places // group),
        table,
        specs=[SMEM] + [pl.BlockSpec()] * 5,
        scratch=[pltpu.VMEM((slice_dev * topics, vocab_shard), F32)],
    )
    swap = [(i, i ^ 1) for i in range(time_peers)]
    recv = lax.ppermute(send, "tm", swap)
    combined = call(
        combine_kernel,
        shape((chips, topics, half), BF16),
        where,
        coef,
        keep,
        recv,
        specs=[SMEM] + [pl.BlockSpec()] * 3,
    )
    far = lax.all_to_all(
        combined,
        "tm",
        split_axis=0,
        concat_axis=0,
        tiled=True,
        axis_index_groups=[[2 * i + c for i in range(chips)] for c in range(2)],
    )
    own, other = call(
        smooth_kernel,
        [shape((slice_dev, topics, half), F32)] * 2,
        where,
        coef,
        keep,
        recv,
        far,
        specs=[SMEM] + [pl.BlockSpec()] * 4,
    )
    partner = lax.ppermute(other, "tm", swap)
    first = core == 0
    means = jnp.concatenate([jnp.where(first, own, partner), jnp.where(first, partner, own)], axis=2)
    return jnp.swapaxes(means, 1, 2), gamma


def solution(mesh):
    return jax.shard_map(
        per_device,
        mesh=mesh,
        in_specs=(
            P("tm", "doc", None),
            P(("tm", "doc"), None),
            P(("tm", "doc"), None),
            P(("tm", "doc")),
            P(),
            P(),
            P(),
        ),
        out_specs=(P("tm", "doc", None), P(("tm", "doc"), None)),
        check_vma=False,
    )
```

```python
import functools
import math

import jax
import jax.numpy as jnp
from jax import lax
from jax.experimental import pallas as pl
from jax.experimental.pallas import tpu as pltpu
from jax.sharding import PartitionSpec as P

E_ITERS = 4
PSEUDO = 0.1
PRIOR_VAR = 1.0
LOG_PSEUDO = math.log(PSEUDO)
F32, BF16, I32 = jnp.float32, jnp.bfloat16, jnp.int32
NT = (((1,), (1,)), ((), ()))
TN = (((0,), (0,)), ((), ()))
SMEM = pl.BlockSpec(memory_space=pltpu.SMEM)


def iota(shape, axis):
    return lax.broadcasted_iota(I32, shape, axis)


def mm(a, b):
    return jnp.dot(a, b, preferred_element_type=F32)


def mmg(a, b, dims):
    return lax.dot_general(a, b, dims, preferred_element_type=F32)


def call(kernel, out_shape, *args, specs=None, scratch=()):
    specs = specs or [pl.BlockSpec()] * len(args)
    return pl.pallas_call(kernel, out_shape=out_shape, in_specs=specs, scratch_shapes=scratch)(*args)


def shape(dims, dtype):
    return jax.ShapeDtypeStruct(dims, dtype)


def place_kernel(peers, capacity, shift, per, slice_ref, where_ref, ids_ref, counts_ref, code_ref, doc_ref, count_ref):
    docs, width = ids_ref.shape
    ids = ids_ref[...]
    owner = lax.shift_right_logical(ids, shift)
    word = ids & ((1 << shift) - 1)
    low = (word & 255).astype(F32)
    high = (lax.shift_right_logical(word, 8) + 1).astype(F32)
    counts = counts_ref[...].astype(F32)
    base = (where_ref[0] * 2 + where_ref[1]) * per
    before = (iota((width, width), 0) < iota((width, width), 1)).astype(F32).astype(BF16)
    owners = iota((peers, width), 0)
    ranks = iota((capacity, width), 0).astype(F32)
    hot = [(owners == owner[d : d + 1, :]).astype(F32) for d in range(docs)]
    inside = mm(jnp.concatenate(hot, axis=0).astype(BF16), before)
    start = jnp.zeros((peers, 1), F32)
    left, right = [], []
    for d in range(docs):
        mine = hot[d]
        part = ((slice_ref[d] - base) << (shift - 8)).astype(F32)
        rank = jnp.sum(mine * (inside[d * peers : (d + 1) * peers] + start), axis=0, keepdims=True)
        start = start + jnp.sum(mine, axis=1, keepdims=True)
        right.append((ranks == rank).astype(F32).astype(BF16))
        left.append(
            jnp.concatenate(
                [
                    mine * low[d : d + 1],
                    mine * (high[d : d + 1] + part),
                    mine * float(d),
                    mine * counts[d : d + 1],
                ],
                axis=0,
            ).astype(BF16)
        )
    placed = mmg(jnp.concatenate(left, axis=1), jnp.concatenate(right, axis=1), NT)
    low_p, high_p, doc_p, count_p = (placed[i * peers : (i + 1) * peers] for i in range(4))
    code_ref[...] = doc_p * 8192.0 + high_p * 256.0 + low_p
    doc_ref[...] = jnp.where(high_p > 0.5, doc_p, -1.0)
    count_ref[...] = count_p


HEAD = 128


def at_of(code):
    return (code & 8191) - 256


def word_of(code, shift):
    return at_of(code) & ((1 << shift) - 1)


def part_of(code, shift):
    return lax.shift_right_logical(at_of(code), shift) & 1


def flatten(flat_ref, rows_ref, group):
    capacity = rows_ref.shape[1]
    for s in range(rows_ref.shape[0]):
        g, i = divmod(s, group)
        flat_ref[g : g + 1, i * capacity : (i + 1) * capacity] = rows_ref[s : s + 1, :]


def tiles(count, grid, low, high):
    return [jnp.where(grid == jnp.where(high == float(h), low, -1.0).astype(BF16), 1.0, 0.0).astype(BF16) for h in range(count)]


def columns(source, code, shift):
    rows, words = source.shape[0] // 2, source.shape[1]
    chunk = 256
    grid = iota((256, chunk), 0).astype(F32).astype(BF16)
    out = []
    for c in range(code.shape[1] // chunk):
        mine = code[:, c * chunk : (c + 1) * chunk]
        word = word_of(mine, shift)
        low, high = (word & 255).astype(F32), lax.shift_right_logical(word, 8).astype(F32)
        both = mm(source[...], jnp.concatenate(tiles(words // 256, grid, low, high), axis=0))
        out.append(jnp.where(part_of(mine, shift) == 0, both[:rows], both[rows:]))
    return jnp.concatenate(out, axis=1)


def fetch_kernel(shift, beta_ref, norm_ref, asked_ref, table_ref, out_ref, flat_ref):
    rows, words = beta_ref.shape
    topics = rows // 2
    tail = topics - HEAD
    peers, capacity = asked_ref.shape
    groups = flat_ref.shape[0]
    group = peers // groups
    norm = jnp.transpose(jnp.broadcast_to(norm_ref[...], (8, norm_ref.shape[1])))[:, 0:1]
    step = 40
    for r in range(0, rows, step):
        table_ref[r : r + step, :] = jnp.exp(beta_ref[r : r + step, :] - norm[r : r + step]).astype(BF16)
    flatten(flat_ref, asked_ref, group)
    third = tail // 3
    spare = capacity - HEAD

    def one(g, carry):
        got = columns(table_ref, flat_ref[pl.ds(g, 1), :].astype(I32), shift)
        wide = jnp.transpose(got[:HEAD]).astype(BF16)
        for i in range(group):
            mine = got[HEAD:, i * capacity : (i + 1) * capacity]
            rest = [mine[b * third : (b + 1) * third, HEAD:] for b in range(3)]
            rest.append(jnp.zeros((third, HEAD - 3 * spare), F32))
            out_ref[g * group + i, 0:capacity, :] = wide[i * capacity : (i + 1) * capacity]
            out_ref[g * group + i, capacity : capacity + tail, :] = mine[:, :HEAD].astype(BF16)
            out_ref[g * group + i, capacity + tail :, :] = jnp.concatenate(rest, axis=1).astype(BF16)
        return carry

    lax.fori_loop(0, groups, one, 0)


def hot_kernel(shift, docs, asked_ref, hot_ref, mask_ref, flat_ref):
    peers, capacity = asked_ref.shape
    groups, places = flat_ref.shape
    group = peers // groups
    step = pl.program_id(0)

    @pl.when(step == 0)
    def _():
        flatten(flat_ref, asked_ref, group)

    code = flat_ref[pl.ds(step, 1), :].astype(I32)
    lane = iota((1, places), 1)
    key = jnp.where(code == 0, -1, lax.shift_right_logical(code, 13))
    for s in range(1, group):
        key = key + jnp.where(lane >= s * capacity, jnp.where(code == 0, 0, docs), 0)
    mask_ref[...] = (iota((group * docs, places), 0) == key).astype(F32).astype(BF16)
    word = word_of(code, shift).astype(F32)
    column = jnp.transpose(jnp.broadcast_to(word, (8, places)))[:, 0:1].astype(I32)
    chunk = 256

    def one(j, carry):
        at = pl.ds(pl.multiple_of(j * chunk, chunk), chunk)
        hot_ref[:, at] = (iota((places, chunk), 1) + j * chunk == column).astype(F32).astype(BF16)
        return carry

    lax.fori_loop(0, hot_ref.shape[1] // chunk, one, 0)


def digamma(value):
    correction = jnp.zeros_like(value)
    for j in range(6):
        correction = correction + 1.0 / (value + float(j))
    shifted = value + 6.0
    inverse = 1.0 / shifted
    square = inverse * inverse
    series = square * (1.0 / 12.0 - square * (1.0 / 120.0 - square * (1.0 / 252.0)))
    return jnp.log(shifted) - 0.5 * inverse - series - correction


def split(value):
    high = value.astype(BF16)
    return high, (value - high.astype(F32)).astype(BF16)


def estep_kernel(
    got_ref, doc_rows, count_rows, counts_ref, dirichlet_ref, gamma_ref, out_ref, head_ref, wide_ref, tail_ref, doc_ref, count_ref
):
    docs = counts_ref.shape[0]
    topics = dirichlet_ref.shape[1]
    tail = topics - HEAD
    third = tail // 3
    peers, capacity = doc_rows.shape
    spare = capacity - HEAD
    flatten(doc_ref, doc_rows, peers)
    flatten(count_ref, count_rows, peers)
    for s in range(peers):
        at = s * capacity
        head_ref[at : at + capacity, :] = got_ref[s, :capacity, :]
        wide_ref[:, at : at + HEAD] = got_ref[s, capacity : capacity + tail, :].astype(F32)
        left = got_ref[s, capacity + tail :, :].astype(F32)
        for b in range(3):
            wide_ref[b * third : (b + 1) * third, at + HEAD : at + capacity] = left[:, b * spare : (b + 1) * spare]
    tail_ref[...] = wide_ref[...].astype(BF16)
    dirichlet = dirichlet_ref[...]
    total = jnp.sum(counts_ref[...].astype(F32), axis=1, keepdims=True)
    gamma = dirichlet + total / float(topics)
    doc = doc_ref[...]
    mask = iota((docs, doc.shape[1]), 0) == doc.astype(I32)
    for step in range(E_ITERS):
        theta = jnp.exp(digamma(gamma) - digamma(jnp.sum(gamma, axis=1, keepdims=True)))
        both = jnp.concatenate(split(theta), axis=0)
        norm = mmg(both[:, :HEAD], head_ref[...], NT) + mm(both[:, HEAD:], tail_ref[...])
        norm = norm[:docs] + norm[docs:]
        norm = jnp.sum(jnp.where(mask, norm, 0.0), axis=0, keepdims=True)
        ratio = jnp.where(doc >= 0.0, count_ref[...] / norm, 0.0)
        high, low = split(ratio)
        high, low = high.astype(F32), low.astype(F32)
        spread = jnp.concatenate([jnp.where(mask, high, 0.0), jnp.where(mask, low, 0.0)], axis=0).astype(BF16)
        part = jnp.concatenate([mm(spread, head_ref[...]), mmg(spread, tail_ref[...], NT)], axis=1)
        gamma = dirichlet + theta * (part[:docs] + part[docs:])
    gamma_ref[...] = gamma
    turned = jnp.transpose(jnp.concatenate([theta[:, HEAD:], jnp.zeros((docs, 2 * HEAD - topics), F32)], axis=1))
    turned = [turned[b * third : (b + 1) * third, :] for b in range(3)]
    turned.append(jnp.zeros((third, HEAD - 3 * docs), F32))
    common = jnp.concatenate([theta[:, :HEAD], jnp.concatenate(turned, axis=1)], axis=0).astype(BF16)
    pad = jnp.zeros((1, HEAD - spare), F32)
    blank = jnp.zeros((4, HEAD), F32)
    for s in range(peers):
        at = s * capacity
        rows = []
        for piece in (high, low):
            rows.append(piece[:, at : at + HEAD])
            rows.append(jnp.concatenate([piece[:, at + HEAD : at + capacity], pad], axis=1))
        out_ref[s, 0 : docs + third, :] = common
        out_ref[s, docs + third : docs + third + 8, :] = jnp.concatenate(rows + [blank], axis=0).astype(BF16)


def stats_kernel(
    shift, docs, core_ref, factor_ref, asked_ref, table_ref, hot_ref, mask_ref, keep_ref, send_ref, total_ref, part_ref, ratio_ref
):
    step = pl.program_id(0)
    steps = pl.num_programs(0)
    group, capacity = asked_ref.shape
    rows, words = table_ref.shape
    topics = rows // 2
    tail = topics - HEAD
    third = tail // 3
    spare = capacity - HEAD
    flatten(part_ref, asked_ref, group)
    turned = []
    for s in range(group):
        block = factor_ref[s, docs : docs + third + 8, :].astype(F32)
        turned.append(jnp.concatenate([block[:third, b * docs : (b + 1) * docs] for b in range(3)], axis=0))
        ratio = block[third : third + 2] + block[third + 2 : third + 4]
        ratio_ref[0:1, s * capacity : s * capacity + HEAD] = ratio[0:1]
        ratio_ref[0:1, s * capacity + HEAD : (s + 1) * capacity] = ratio[1:2, :spare]
    mask = mask_ref[...]
    top = factor_ref[:, :docs, :].reshape(group * docs, HEAD)
    bottom = jnp.concatenate(turned, axis=1).astype(BF16)
    factor = jnp.concatenate([mmg(top, mask, TN), mm(bottom, mask)], axis=0) * ratio_ref[...]
    part = part_of(part_ref[...].astype(I32), shift)
    factor = jnp.concatenate([jnp.where(part == 0, factor, 0.0), jnp.where(part == 1, factor, 0.0)], axis=0).astype(BF16)
    chunk = 256
    for j in range(words // chunk):
        new = mm(factor, hot_ref[:, j * chunk : (j + 1) * chunk])

        @pl.when(step == 0)
        def _():
            total_ref[:, j * chunk : (j + 1) * chunk] = new

        @pl.when(step > 0)
        def _():
            total_ref[:, j * chunk : (j + 1) * chunk] += new

    @pl.when(step == steps - 1)
    def _():
        half = words // 2
        first = core_ref[0] == 0
        size = 16

        def finish(i, carry):
            at = pl.ds(pl.multiple_of(i * size, size), size)
            shifted = jnp.log(1.0 + (1.0 / PSEUDO) * (table_ref[at, :].astype(F32) * total_ref[at, :]))
            left, right = shifted[:, :half], shifted[:, half:]
            keep_ref[at, :] = jnp.where(first, left, right)
            send_ref[at, :] = jnp.where(first, right, left)
            return carry

        lax.fori_loop(0, rows // size, finish, 0)


G0, S0, H0, B0, PHI0, QK, KNEXT, PHI, WF0, WQ0, NCOEF = 0, 4, 8, 12, 16, 20, 21, 22, 23, 27, 32


def coef_kernel(chips, chip_ref, drift_ref, obs_ref, out_ref, rows_ref):
    per = 4
    length = chips * per
    drift, obs = drift_ref[...], obs_ref[...]
    one, zero = jnp.ones_like(drift), jnp.zeros_like(drift)
    var = one * PRIOR_VAR
    gain, smooth = [], []
    for t in range(length):
        pred = var + drift
        now = pred / (pred + obs)
        var = (1.0 - now) * pred
        gain.append(now)
        smooth.append(var / (var + drift) if t < length - 1 else zero)
    level, forward = zero, []
    for t in range(length):
        level = (1.0 - gain[t]) * level + gain[t]
        forward.append(level)
    ones_smoothed = [None] * length
    level = zero
    for t in reversed(range(length)):
        level = (1.0 - smooth[t]) * forward[t] + smooth[t] * level
        ones_smoothed[t] = level
    beta, phi, sigma, kappa = [], [], [], []
    for c in range(chips):
        run, back, k = one, one, zero
        for t in range(c * per, (c + 1) * per):
            run = run * (1.0 - gain[t])
            phi.append(run)
            beta.append(back * (1.0 - smooth[t]))
            k = k + beta[t] * run
            back = back * smooth[t]
        sigma.append(back)
        kappa.append(k)
    total = [phi[c * per + per - 1] for c in range(chips)]
    lead = [zero] * (chips + 1)
    for c in reversed(range(chips)):
        lead[c] = kappa[c] + sigma[c] * lead[c + 1] * total[c]
    chip = chip_ref[0]
    for c in range(chips):
        rows = [None] * NCOEF
        for u in range(per):
            t = c * per + u
            rows[G0 + u], rows[S0 + u], rows[H0 + u] = gain[t], smooth[t], ones_smoothed[t] * LOG_PSEUDO
            rows[B0 + u], rows[PHI0 + u] = beta[t], phi[t]
        rows[QK], rows[KNEXT], rows[PHI] = sigma[c] * lead[c + 1], lead[c + 1], total[c]
        for j in range(chips):
            behind, ahead = zero, zero
            if j < c:
                behind = one
                for m in range(j + 1, c):
                    behind = behind * total[m]
            if j > c:
                ahead = one
                for m in range(c + 1, j):
                    ahead = ahead * sigma[m]
            rows[WF0 + j], rows[WQ0 + j] = behind, ahead

        @pl.when(chip == c)
        def _():
            for r in range(NCOEF):
                rows_ref[r : r + 1, : drift.shape[1]] = zero if rows[r] is None else rows[r]

    out_ref[...] = jnp.transpose(rows_ref[...])[: out_ref.shape[0]]


def local_filter(coef, values):
    out, level = [], None
    for u in range(4):
        gain = coef[:, G0 + u : G0 + u + 1]
        level = gain * values[u] if level is None else (1.0 - gain) * level + gain * values[u]
        out.append(level)
    return out


def four(first, keep_ref, recv_ref, topics, at):
    own = [keep_ref[pl.ds(u * topics + at, 8), :] for u in range(2)]
    other = [recv_ref[pl.ds(u * topics + at, 8), :] for u in range(2)]
    return [jnp.where(first, own[u], other[u]) for u in range(2)] + [
        jnp.where(first, other[u], own[u]) for u in range(2)
    ]


def combine_kernel(where_ref, coef_ref, keep_ref, recv_ref, out_ref):
    chips, topics, _ = out_ref.shape
    first, chip = where_ref[1] == 0, where_ref[0]

    def block(i, carry):
        at = pl.multiple_of(i * 8, 8)
        coef = coef_ref[pl.ds(at, 8), :]
        local = local_filter(coef, four(first, keep_ref, recv_ref, topics, at))
        back = coef[:, QK : QK + 1] * local[3]
        for u in range(4):
            back = back + coef[:, B0 + u : B0 + u + 1] * local[u]
        for j in range(chips):
            out_ref[j, pl.ds(at, 8), :] = jnp.where(j > chip, local[3], back).astype(BF16)
        return carry

    lax.fori_loop(0, topics // 8, block, 0)


def edges_kernel(where_ref, coef_ref, keep_ref, recv_ref, far_ref, own_ref, other_ref):
    chips, topics, _ = far_ref.shape
    first = where_ref[1] == 0

    def block(i, carry):
        at = pl.multiple_of(i * 8, 8)
        coef = coef_ref[pl.ds(at, 8), :]

        def take(r):
            return coef[:, r : r + 1]

        local = local_filter(coef, four(first, keep_ref, recv_ref, topics, at))
        entering = jnp.zeros_like(local[0])
        ahead = jnp.zeros_like(local[0])
        for j in range(chips):
            far = far_ref[j, pl.ds(at, 8), :].astype(F32)
            entering = entering + take(WF0 + j) * far
            ahead = ahead + take(WQ0 + j) * far
        after = ahead + take(KNEXT) * (local[3] + take(PHI) * entering)
        middle = after
        for u in (3, 2):
            weight = take(S0 + u)
            middle = (1.0 - weight) * (local[u] + take(PHI0 + u) * entering) + weight * middle
        half = local[1] + take(PHI0 + 1) * entering
        own_ref[0, pl.ds(at, 8), :] = jnp.where(first, entering, half)
        own_ref[1, pl.ds(at, 8), :] = jnp.where(first, middle, after)
        other_ref[0, pl.ds(at, 8), :] = jnp.where(first, half, entering)
        other_ref[1, pl.ds(at, 8), :] = jnp.where(first, after, middle)
        return carry

    lax.fori_loop(0, topics // 8, block, 0)


def means_kernel(where_ref, coef_ref, keep_ref, send_ref, own_ref, other_ref, out_ref):
    _, topics, words = out_ref.shape
    half = words // 2
    first = where_ref[1] == 0

    def block(i, carry):
        at = pl.multiple_of(i * 8, 8)
        coef = coef_ref[pl.ds(at, 8), :]

        def take(r):
            return jnp.where(first, coef[:, r : r + 1], coef[:, r + 2 : r + 3])

        gain, weight, level = ([take(r + u) for u in range(2)] for r in (G0, S0, H0))
        sides = []
        for value_ref, edge_ref in ((keep_ref, own_ref), (send_ref, other_ref)):
            values = [value_ref[pl.ds(u * topics + at, 8), :] for u in range(2)]
            early = (1.0 - gain[0]) * edge_ref[0, pl.ds(at, 8), :] + gain[0] * values[0]
            late = (1.0 - gain[1]) * early + gain[1] * values[1]
            late = (1.0 - weight[1]) * late + weight[1] * edge_ref[1, pl.ds(at, 8), :]
            early = (1.0 - weight[0]) * early + weight[0] * late
            sides.append((early + level[0], late + level[1]))
        for u in range(2):
            out_ref[u, pl.ds(at, 8), :half] = jnp.where(first, sides[0][u], sides[1][u])
            out_ref[u, pl.ds(at, 8), half:] = jnp.where(first, sides[1][u], sides[0][u])
        return carry

    lax.fori_loop(0, topics // 8, block, 0)


def per_device(beta_mean, word_ids, word_counts, doc_slice, dirichlet, drift_var, obs_var):
    slice_dev, vocab_shard, topics = beta_mean.shape
    docs, width = word_ids.shape
    peers = lax.axis_size("doc")
    time_peers = lax.axis_size("tm")
    here = lax.axis_index("tm")
    chip, core = here // 2, here % 2
    chips = time_peers // 2
    shift = vocab_shard.bit_length() - 1
    slots = docs * width
    capacity = slots * 5 // (4 * peers)
    places = peers * capacity
    half = vocab_shard // 2
    rows = slice_dev * topics
    tail = topics - HEAD
    packed = capacity + tail + tail // 3
    groups = 4
    group = peers // groups
    where = jnp.stack([chip, core]).astype(I32)
    vmem = pl.BlockSpec()

    beta = jnp.swapaxes(beta_mean, 1, 2)
    code, doc, count = call(
        functools.partial(place_kernel, peers, capacity, shift, slice_dev),
        [shape((peers, capacity), F32)] * 3,
        doc_slice,
        where,
        word_ids,
        word_counts,
        specs=[SMEM, SMEM, vmem, vmem],
    )
    top = jnp.max(beta, axis=2)
    mass = jnp.sum(jnp.exp(beta - top[:, :, None]), axis=2)
    stats = jnp.concatenate([top.reshape(1, 1, -1), mass.reshape(1, 1, -1)], axis=2)
    outgoing = jnp.concatenate(
        [code.reshape(peers, 1, capacity), jnp.broadcast_to(stats, (peers, 1, stats.shape[2]))], axis=2
    )
    arrived = lax.all_to_all(outgoing, "doc", split_axis=0, concat_axis=0, tiled=True)
    coef = call(
        functools.partial(coef_kernel, chips),
        shape((topics, NCOEF), F32),
        where,
        drift_var.reshape(1, topics),
        obs_var.reshape(1, topics),
        specs=[SMEM, vmem, vmem],
        scratch=[pltpu.VMEM((NCOEF, 2 * HEAD), F32)],
    )
    asked = arrived[:, 0, :capacity]
    tops = arrived[:, 0, capacity : capacity + rows]
    masses = arrived[:, 0, capacity + rows :]
    highest = jnp.max(tops, axis=0)
    log_norm = highest + jnp.log(jnp.sum(masses * jnp.exp(tops - highest), axis=0))
    log_norm = jnp.pad(log_norm, (0, 4 * HEAD - rows)).reshape(1, -1)
    flat = pltpu.VMEM((groups, places // groups), F32)
    table, fetched = call(
        functools.partial(fetch_kernel, shift),
        [shape((rows, vocab_shard), BF16), shape((peers, packed, HEAD), BF16)],
        beta.reshape(rows, vocab_shard),
        log_norm,
        asked,
        scratch=[flat],
    )

    def exchange(value):
        return lax.all_to_all(value, "doc", split_axis=0, concat_axis=0, tiled=True)

    asked_late, fetched = lax.optimization_barrier((asked, fetched))
    got = exchange(fetched)
    hot, mask = pl.pallas_call(
        functools.partial(hot_kernel, shift, docs),
        grid=(groups,),
        out_shape=[shape((places, vocab_shard), BF16), shape((peers * docs, places // groups), BF16)],
        in_specs=[pl.BlockSpec((peers, capacity), lambda g: (0, 0))],
        out_specs=[
            pl.BlockSpec((places // groups, vocab_shard), lambda g: (g, 0)),
            pl.BlockSpec((group * docs, places // groups), lambda g: (g, 0)),
        ],
        scratch_shapes=[flat],
    )(asked_late)
    got, hot, mask = lax.optimization_barrier((got, hot, mask))
    line = pltpu.VMEM((1, places), F32)
    gamma, factors = call(
        estep_kernel,
        [shape((docs, topics), F32), shape((peers, docs + tail // 3 + 8, HEAD), BF16)],
        got,
        doc,
        count,
        word_counts,
        dirichlet.reshape(1, topics),
        scratch=[pltpu.VMEM((places, HEAD), BF16), pltpu.VMEM((tail, places), F32), pltpu.VMEM((tail, places), BF16), line, line],
    )
    factors = exchange(factors)
    line = pltpu.VMEM((1, places // groups), F32)
    keep, send = pl.pallas_call(
        functools.partial(stats_kernel, shift, docs),
        grid=(groups,),
        out_shape=[shape((rows, half), F32)] * 2,
        in_specs=[
            SMEM,
            pl.BlockSpec((group,) + factors.shape[1:], lambda g: (g, 0, 0)),
            pl.BlockSpec((group, capacity), lambda g: (g, 0)),
            pl.BlockSpec((rows, vocab_shard), lambda g: (0, 0)),
            pl.BlockSpec((places // groups, vocab_shard), lambda g: (g, 0)),
            pl.BlockSpec((group * docs, places // groups), lambda g: (g, 0)),
        ],
        out_specs=[pl.BlockSpec((rows, half), lambda g: (0, 0))] * 2,
        scratch_shapes=[pltpu.VMEM((rows, vocab_shard), F32), line, line],
    )(core.astype(I32).reshape(1), factors, asked, table, hot, mask)
    swap = [(i, i ^ 1) for i in range(time_peers)]
    recv = lax.ppermute(send, "tm", swap)
    combined = call(
        combine_kernel,
        shape((chips, topics, half), BF16),
        where,
        coef,
        keep,
        recv,
        specs=[SMEM] + [vmem] * 3,
    )
    far = lax.all_to_all(
        combined,
        "tm",
        split_axis=0,
        concat_axis=0,
        tiled=True,
        axis_index_groups=[[2 * i + c for i in range(chips)] for c in range(2)],
    )
    own, other = call(
        edges_kernel,
        [shape((slice_dev, topics, half), F32)] * 2,
        where,
        coef,
        keep,
        recv,
        far,
        specs=[SMEM] + [vmem] * 4,
    )
    partner = lax.ppermute(other, "tm", swap)
    means = call(
        means_kernel,
        shape((slice_dev, topics, vocab_shard), F32),
        where,
        coef,
        keep,
        send,
        own,
        partner,
        specs=[SMEM] + [vmem] * 5,
    )
    return jnp.swapaxes(means, 1, 2), gamma


def solution(mesh):
    return jax.shard_map(
        per_device,
        mesh=mesh,
        in_specs=(
            P("tm", "doc", None),
            P(("tm", "doc"), None),
            P(("tm", "doc"), None),
            P(("tm", "doc")),
            P(),
            P(),
            P(),
        ),
        out_specs=(P("tm", "doc", None), P(("tm", "doc"), None)),
        check_vma=False,
    )
```

```python
import functools
import math

import jax
import jax.numpy as jnp
from jax import lax
from jax.experimental import pallas as pl
from jax.experimental.pallas import tpu as pltpu
from jax.sharding import PartitionSpec as P

E_ITERS = 4
PSEUDO = 0.1
PRIOR_VAR = 1.0
LOG_PSEUDO = math.log(PSEUDO)
F32, BF16, I32 = jnp.float32, jnp.bfloat16, jnp.int32
NT = (((1,), (1,)), ((), ()))
TN = (((0,), (0,)), ((), ()))
SMEM = pl.BlockSpec(memory_space=pltpu.SMEM)


def iota(shape, axis):
    return lax.broadcasted_iota(I32, shape, axis)


def mm(a, b):
    return jnp.dot(a, b, preferred_element_type=F32)


def mmg(a, b, dims):
    return lax.dot_general(a, b, dims, preferred_element_type=F32)


VMEM = pl.BlockSpec(memory_space=pltpu.VMEM)


def shape(dims, dtype):
    return jax.ShapeDtypeStruct(dims, dtype)


def call(kernel, outs, *args, scalars=0, scratch=()):
    args = args[:scalars] + tuple(pltpu.with_memory_space_constraint(a, pltpu.VMEM) for a in args[scalars:])
    return pl.pallas_call(
        kernel,
        out_shape=outs,
        in_specs=[SMEM] * scalars + [VMEM] * (len(args) - scalars),
        out_specs=[VMEM if isinstance(o, pl.MemoryRef) else pl.BlockSpec() for o in outs],
        scratch_shapes=scratch,
        compiler_params=pltpu.CompilerParams(vmem_limit_bytes=36 << 20),
    )(*args)


def place_kernel(peers, capacity, shift, per, slice_ref, where_ref, ids_ref, counts_ref, code_ref, doc_ref, count_ref):
    docs, width = ids_ref.shape
    ids = ids_ref[...]
    owner = lax.shift_right_logical(ids, shift)
    word = ids & ((1 << shift) - 1)
    low = (word & 255).astype(F32)
    high = (lax.shift_right_logical(word, 8) + 1).astype(F32)
    counts = counts_ref[...].astype(F32)
    base = (where_ref[0] * 2 + where_ref[1]) * per
    before = (iota((width, width), 0) < iota((width, width), 1)).astype(F32).astype(BF16)
    owners = iota((peers, width), 0)
    ranks = iota((capacity, width), 0).astype(F32)
    hot = [(owners == owner[d : d + 1, :]).astype(F32) for d in range(docs)]
    inside = mm(jnp.concatenate(hot, axis=0).astype(BF16), before)
    start = jnp.zeros((peers, 1), F32)
    left, right = [], []
    for d in range(docs):
        mine = hot[d]
        part = ((slice_ref[d] - base) << (shift - 8)).astype(F32)
        rank = jnp.sum(mine * (inside[d * peers : (d + 1) * peers] + start), axis=0, keepdims=True)
        start = start + jnp.sum(mine, axis=1, keepdims=True)
        right.append((ranks == rank).astype(F32).astype(BF16))
        left.append(
            jnp.concatenate(
                [
                    mine * low[d : d + 1],
                    mine * (high[d : d + 1] + part),
                    mine * float(d),
                    mine * counts[d : d + 1],
                ],
                axis=0,
            ).astype(BF16)
        )
    placed = mmg(jnp.concatenate(left, axis=1), jnp.concatenate(right, axis=1), NT)
    low_p, high_p, doc_p, count_p = (placed[i * peers : (i + 1) * peers] for i in range(4))
    code_ref[...] = doc_p * 8192.0 + high_p * 256.0 + low_p
    doc_ref[...] = jnp.where(high_p > 0.5, doc_p, -1.0)
    count_ref[...] = count_p


HEAD = 128


def at_of(code):
    return (code & 8191) - 256


def word_of(code, shift):
    return at_of(code) & ((1 << shift) - 1)


def part_of(code, shift):
    return lax.shift_right_logical(at_of(code), shift) & 1


def flatten(flat_ref, rows_ref, group):
    capacity = rows_ref.shape[1]
    for s in range(rows_ref.shape[0]):
        g, i = divmod(s, group)
        flat_ref[g : g + 1, i * capacity : (i + 1) * capacity] = rows_ref[s : s + 1, :]


def tiles(count, grid, low, high):
    return [jnp.where(grid == jnp.where(high == float(h), low, -1.0).astype(BF16), 1.0, 0.0).astype(BF16) for h in range(count)]


def columns(source, code, shift):
    rows, words = source.shape[0] // 2, source.shape[1]
    chunk = 256
    grid = iota((256, chunk), 0).astype(F32).astype(BF16)
    out = []
    for c in range(code.shape[1] // chunk):
        mine = code[:, c * chunk : (c + 1) * chunk]
        word = word_of(mine, shift)
        low, high = (word & 255).astype(F32), lax.shift_right_logical(word, 8).astype(F32)
        both = mm(source[...], jnp.concatenate(tiles(words // 256, grid, low, high), axis=0))
        out.append(jnp.where(part_of(mine, shift) == 0, both[:rows], both[rows:]))
    return jnp.concatenate(out, axis=1)


def fetch_kernel(shift, beta_ref, norm_ref, asked_ref, table_ref, out_ref, flat_ref):
    rows, words = beta_ref.shape
    topics = rows // 2
    tail = topics - HEAD
    peers, capacity = asked_ref.shape
    groups = flat_ref.shape[0]
    group = peers // groups
    norm = jnp.transpose(jnp.broadcast_to(norm_ref[...], (8, norm_ref.shape[1])))[:, 0:1]
    step = 40
    for r in range(0, rows, step):
        table_ref[r : r + step, :] = jnp.exp(beta_ref[r : r + step, :] - norm[r : r + step]).astype(BF16)
    flatten(flat_ref, asked_ref, group)
    third = tail // 3
    spare = capacity - HEAD

    def one(g, carry):
        got = columns(table_ref, flat_ref[pl.ds(g, 1), :].astype(I32), shift)
        wide = jnp.transpose(got[:HEAD]).astype(BF16)
        for i in range(group):
            mine = got[HEAD:, i * capacity : (i + 1) * capacity]
            rest = [mine[b * third : (b + 1) * third, HEAD:] for b in range(3)]
            rest.append(jnp.zeros((third, HEAD - 3 * spare), F32))
            out_ref[g * group + i, 0:capacity, :] = wide[i * capacity : (i + 1) * capacity]
            out_ref[g * group + i, capacity : capacity + tail, :] = mine[:, :HEAD].astype(BF16)
            out_ref[g * group + i, capacity + tail :, :] = jnp.concatenate(rest, axis=1).astype(BF16)
        return carry

    lax.fori_loop(0, groups, one, 0)


def index_kernel(shift, docs, asked_ref, low_ref, block_ref, mask_ref, flat_ref):
    peers, capacity = asked_ref.shape
    groups, places = flat_ref.shape
    group = peers // groups
    flatten(flat_ref, asked_ref, group)
    lane = iota((1, places), 1)
    chunk = low_ref.shape[1]
    grid = iota((places, chunk), 1).astype(F32).astype(BF16)
    for g in range(groups):
        code = flat_ref[g : g + 1, :].astype(I32)
        key = jnp.where(code == 0, -1, lax.shift_right_logical(code, 13))
        for s in range(1, group):
            key = key + jnp.where(lane >= s * capacity, jnp.where(code == 0, 0, docs), 0)
        mask_ref[g * group * docs : (g + 1) * group * docs, :] = (
            (iota((group * docs, places), 0) == key).astype(F32).astype(BF16)
        )
        at = at_of(code) & ((2 << shift) - 1)
        low = (at & (chunk - 1)).astype(F32)
        block_ref[:, g * places : (g + 1) * places] = lax.shift_right_logical(at, chunk.bit_length() - 1).astype(F32)
        column = jnp.transpose(jnp.broadcast_to(low, (8, places)))[:, 0:1].astype(BF16)
        low_ref[g * places : (g + 1) * places, :] = jnp.where(grid == column, 1.0, 0.0).astype(BF16)


def digamma(value):
    correction = jnp.zeros_like(value)
    for j in range(6):
        correction = correction + 1.0 / (value + float(j))
    shifted = value + 6.0
    inverse = 1.0 / shifted
    square = inverse * inverse
    series = square * (1.0 / 12.0 - square * (1.0 / 120.0 - square * (1.0 / 252.0)))
    return jnp.log(shifted) - 0.5 * inverse - series - correction


def split(value):
    high = value.astype(BF16)
    return high, (value - high.astype(F32)).astype(BF16)


def estep_kernel(
    got_ref, doc_rows, count_rows, counts_ref, dirichlet_ref, gamma_ref, out_ref, head_ref, wide_ref, tail_ref, doc_ref, count_ref
):
    docs = counts_ref.shape[0]
    topics = dirichlet_ref.shape[1]
    tail = topics - HEAD
    third = tail // 3
    peers, capacity = doc_rows.shape
    spare = capacity - HEAD
    flatten(doc_ref, doc_rows, peers)
    flatten(count_ref, count_rows, peers)
    for s in range(peers):
        at = s * capacity
        head_ref[at : at + capacity, :] = got_ref[s, :capacity, :]
        wide_ref[:, at : at + HEAD] = got_ref[s, capacity : capacity + tail, :].astype(F32)
        left = got_ref[s, capacity + tail :, :].astype(F32)
        for b in range(3):
            wide_ref[b * third : (b + 1) * third, at + HEAD : at + capacity] = left[:, b * spare : (b + 1) * spare]
    tail_ref[...] = wide_ref[...].astype(BF16)
    dirichlet = dirichlet_ref[...]
    total = jnp.sum(counts_ref[...].astype(F32), axis=1, keepdims=True)
    gamma = dirichlet + total / float(topics)
    doc = doc_ref[...]
    mask = iota((docs, doc.shape[1]), 0) == doc.astype(I32)
    for step in range(E_ITERS):
        theta = jnp.exp(digamma(gamma) - digamma(jnp.sum(gamma, axis=1, keepdims=True)))
        both = jnp.concatenate(split(theta), axis=0)
        norm = mmg(both[:, :HEAD], head_ref[...], NT) + mm(both[:, HEAD:], tail_ref[...])
        norm = norm[:docs] + norm[docs:]
        norm = jnp.sum(jnp.where(mask, norm, 0.0), axis=0, keepdims=True)
        ratio = jnp.where(doc >= 0.0, count_ref[...] / norm, 0.0)
        high, low = split(ratio)
        high, low = high.astype(F32), low.astype(F32)
        spread = jnp.concatenate([jnp.where(mask, high, 0.0), jnp.where(mask, low, 0.0)], axis=0).astype(BF16)
        part = jnp.concatenate([mm(spread, head_ref[...]), mmg(spread, tail_ref[...], NT)], axis=1)
        gamma = dirichlet + theta * (part[:docs] + part[docs:])
    gamma_ref[...] = gamma
    turned = jnp.transpose(jnp.concatenate([theta[:, HEAD:], jnp.zeros((docs, 2 * HEAD - topics), F32)], axis=1))
    turned = [turned[b * third : (b + 1) * third, :] for b in range(3)]
    turned.append(jnp.zeros((third, HEAD - 3 * docs), F32))
    common = jnp.concatenate([theta[:, :HEAD], jnp.concatenate(turned, axis=1)], axis=0).astype(BF16)
    pad = jnp.zeros((1, HEAD - spare), F32)
    blank = jnp.zeros((4, HEAD), F32)
    for s in range(peers):
        at = s * capacity
        rows = []
        for piece in (high, low):
            rows.append(piece[:, at : at + HEAD])
            rows.append(jnp.concatenate([piece[:, at + HEAD : at + capacity], pad], axis=1))
        out_ref[s, 0 : docs + third, :] = common
        out_ref[s, docs + third : docs + third + 8, :] = jnp.concatenate(rows + [blank], axis=0).astype(BF16)


def factor_of(docs, capacity, factor_in, mask_ref, ratio_ref, out_ref):
    peers = factor_in.shape[0]
    topics, places = out_ref.shape[0], mask_ref.shape[1]
    group = places // capacity
    third = (topics - HEAD) // 3
    spare = capacity - HEAD
    for g in range(peers // group):
        turned = []
        for i in range(group):
            block = factor_in[g * group + i, docs : docs + third + 8, :].astype(F32)
            turned.append(jnp.concatenate([block[:third, b * docs : (b + 1) * docs] for b in range(3)], axis=0))
            ratio = block[third : third + 2] + block[third + 2 : third + 4]
            ratio_ref[0:1, i * capacity : i * capacity + HEAD] = ratio[0:1]
            ratio_ref[0:1, i * capacity + HEAD : (i + 1) * capacity] = ratio[1:2, :spare]
        mask = mask_ref[g * group * docs : (g + 1) * group * docs, :]
        top = factor_in[g * group : (g + 1) * group, :docs, :].reshape(group * docs, HEAD)
        bottom = jnp.concatenate(turned, axis=1).astype(BF16)
        at = slice(g * places, (g + 1) * places)
        ratio = ratio_ref[...]
        out_ref[:HEAD, at] = (mmg(top, mask, TN) * ratio).astype(BF16)
        out_ref[HEAD:, at] = (mm(bottom, mask) * ratio).astype(BF16)


def half_stats(half, factor_ref, low_ref, block_ref, table_ref, out_ref):
    topics = factor_ref.shape[0]
    parts = table_ref.shape[0] // topics
    chunk = low_ref.shape[1]
    blocks = table_ref.shape[1] // chunk
    block = block_ref[...]
    for t in range(parts):
        for q in range(blocks // 2):
            h = half * (blocks // 2) + q
            here = jnp.where(block == (t * blocks + h).astype(F32), 1.0, 0.0).astype(BF16)
            total = mm(factor_ref[...] * here, low_ref[...])
            words = pl.ds(pl.multiple_of(h * chunk, chunk), chunk)
            table = table_ref[t * topics : (t + 1) * topics, words].astype(F32)
            out_ref[t * topics : (t + 1) * topics, q * chunk : (q + 1) * chunk] = jnp.log(
                1.0 + (1.0 / PSEUDO) * (table * total)
            )


def send_kernel(
    docs, capacity, where_ref, factor_in, mask_ref, low_ref, block_ref, table_ref, out_ref, factor_ref, ratio_ref
):
    factor_of(docs, capacity, factor_in, mask_ref, ratio_ref, factor_ref)
    half_stats(1 - where_ref[1], factor_ref, low_ref, block_ref, table_ref, out_ref)


def keep_kernel(where_ref, factor_ref, low_ref, block_ref, table_ref, out_ref):
    half_stats(where_ref[1], factor_ref, low_ref, block_ref, table_ref, out_ref)


G0, S0, H0, B0, PHI0, QK, KNEXT, PHI, WF0, WQ0, NCOEF = 0, 4, 8, 12, 16, 20, 21, 22, 23, 27, 32


def coef_kernel(chips, chip_ref, drift_ref, obs_ref, out_ref, rows_ref):
    per = 4
    length = chips * per
    drift, obs = drift_ref[...], obs_ref[...]
    one, zero = jnp.ones_like(drift), jnp.zeros_like(drift)
    var = one * PRIOR_VAR
    gain, smooth = [], []
    for t in range(length):
        pred = var + drift
        now = pred / (pred + obs)
        var = (1.0 - now) * pred
        gain.append(now)
        smooth.append(var / (var + drift) if t < length - 1 else zero)
    level, forward = zero, []
    for t in range(length):
        level = (1.0 - gain[t]) * level + gain[t]
        forward.append(level)
    ones_smoothed = [None] * length
    level = zero
    for t in reversed(range(length)):
        level = (1.0 - smooth[t]) * forward[t] + smooth[t] * level
        ones_smoothed[t] = level
    beta, phi, sigma, kappa = [], [], [], []
    for c in range(chips):
        run, back, k = one, one, zero
        for t in range(c * per, (c + 1) * per):
            run = run * (1.0 - gain[t])
            phi.append(run)
            beta.append(back * (1.0 - smooth[t]))
            k = k + beta[t] * run
            back = back * smooth[t]
        sigma.append(back)
        kappa.append(k)
    total = [phi[c * per + per - 1] for c in range(chips)]
    lead = [zero] * (chips + 1)
    for c in reversed(range(chips)):
        lead[c] = kappa[c] + sigma[c] * lead[c + 1] * total[c]
    chip = chip_ref[0]
    for c in range(chips):
        rows = [None] * NCOEF
        for u in range(per):
            t = c * per + u
            rows[G0 + u], rows[S0 + u], rows[H0 + u] = gain[t], smooth[t], ones_smoothed[t] * LOG_PSEUDO
            rows[B0 + u], rows[PHI0 + u] = beta[t], phi[t]
        rows[QK], rows[KNEXT], rows[PHI] = sigma[c] * lead[c + 1], lead[c + 1], total[c]
        for j in range(chips):
            behind, ahead = zero, zero
            if j < c:
                behind = one
                for m in range(j + 1, c):
                    behind = behind * total[m]
            if j > c:
                ahead = one
                for m in range(c + 1, j):
                    ahead = ahead * sigma[m]
            rows[WF0 + j], rows[WQ0 + j] = behind, ahead

        @pl.when(chip == c)
        def _():
            for r in range(NCOEF):
                rows_ref[r : r + 1, : drift.shape[1]] = zero if rows[r] is None else rows[r]

    out_ref[...] = jnp.transpose(rows_ref[...])[: out_ref.shape[0]]


def local_filter(coef, values):
    out, level = [], None
    for u in range(4):
        gain = coef[:, G0 + u : G0 + u + 1]
        level = gain * values[u] if level is None else (1.0 - gain) * level + gain * values[u]
        out.append(level)
    return out


def four(first, keep_ref, recv_ref, topics, at):
    own = [keep_ref[pl.ds(u * topics + at, 8), :] for u in range(2)]
    other = [recv_ref[pl.ds(u * topics + at, 8), :] for u in range(2)]
    return [jnp.where(first, own[u], other[u]) for u in range(2)] + [
        jnp.where(first, other[u], own[u]) for u in range(2)
    ]


def combine_kernel(where_ref, coef_ref, keep_ref, recv_ref, out_ref):
    chips, topics, _ = out_ref.shape
    first, chip = where_ref[1] == 0, where_ref[0]

    def block(i, carry):
        at = pl.multiple_of(i * 8, 8)
        coef = coef_ref[pl.ds(at, 8), :]
        local = local_filter(coef, four(first, keep_ref, recv_ref, topics, at))
        back = coef[:, QK : QK + 1] * local[3]
        for u in range(4):
            back = back + coef[:, B0 + u : B0 + u + 1] * local[u]
        for j in range(chips):
            out_ref[j, pl.ds(at, 8), :] = jnp.where(j > chip, local[3], back).astype(BF16)
        return carry

    lax.fori_loop(0, topics // 8, block, 0, unroll=5)


def edges_kernel(where_ref, coef_ref, keep_ref, recv_ref, far_ref, own_ref, other_ref):
    chips, topics, _ = far_ref.shape
    first = where_ref[1] == 0

    def block(i, carry):
        at = pl.multiple_of(i * 8, 8)
        coef = coef_ref[pl.ds(at, 8), :]

        def take(r):
            return coef[:, r : r + 1]

        local = local_filter(coef, four(first, keep_ref, recv_ref, topics, at))
        entering = jnp.zeros_like(local[0])
        ahead = jnp.zeros_like(local[0])
        for j in range(chips):
            far = far_ref[j, pl.ds(at, 8), :].astype(F32)
            entering = entering + take(WF0 + j) * far
            ahead = ahead + take(WQ0 + j) * far
        after = ahead + take(KNEXT) * (local[3] + take(PHI) * entering)
        middle = after
        for u in (3, 2):
            weight = take(S0 + u)
            middle = (1.0 - weight) * (local[u] + take(PHI0 + u) * entering) + weight * middle
        half = local[1] + take(PHI0 + 1) * entering
        own_ref[0, pl.ds(at, 8), :] = jnp.where(first, entering, half)
        own_ref[1, pl.ds(at, 8), :] = jnp.where(first, middle, after)
        other_ref[0, pl.ds(at, 8), :] = jnp.where(first, half, entering)
        other_ref[1, pl.ds(at, 8), :] = jnp.where(first, after, middle)
        return carry

    lax.fori_loop(0, topics // 8, block, 0, unroll=5)


def means_kernel(where_ref, coef_ref, keep_ref, send_ref, own_ref, other_ref, out_ref):
    _, topics, words = out_ref.shape
    half = words // 2
    first = where_ref[1] == 0

    def block(i, carry):
        at = pl.multiple_of(i * 8, 8)
        coef = coef_ref[pl.ds(at, 8), :]

        def take(r):
            return jnp.where(first, coef[:, r : r + 1], coef[:, r + 2 : r + 3])

        gain, weight, level = ([take(r + u) for u in range(2)] for r in (G0, S0, H0))
        sides = []
        for value_ref, edge_ref in ((keep_ref, own_ref), (send_ref, other_ref)):
            values = [value_ref[pl.ds(u * topics + at, 8), :] for u in range(2)]
            early = (1.0 - gain[0]) * edge_ref[0, pl.ds(at, 8), :] + gain[0] * values[0]
            late = (1.0 - gain[1]) * early + gain[1] * values[1]
            late = (1.0 - weight[1]) * late + weight[1] * edge_ref[1, pl.ds(at, 8), :]
            early = (1.0 - weight[0]) * early + weight[0] * late
            sides.append((early + level[0], late + level[1]))
        for u in range(2):
            out_ref[u, pl.ds(at, 8), :half] = jnp.where(first, sides[0][u], sides[1][u])
            out_ref[u, pl.ds(at, 8), half:] = jnp.where(first, sides[1][u], sides[0][u])
        return carry

    lax.fori_loop(0, topics // 8, block, 0, unroll=5)


def per_device(beta_mean, word_ids, word_counts, doc_slice, dirichlet, drift_var, obs_var):
    slice_dev, vocab_shard, topics = beta_mean.shape
    docs, width = word_ids.shape
    peers = lax.axis_size("doc")
    time_peers = lax.axis_size("tm")
    here = lax.axis_index("tm")
    chip, core = here // 2, here % 2
    chips = time_peers // 2
    shift = vocab_shard.bit_length() - 1
    slots = docs * width
    capacity = slots * 5 // (4 * peers)
    places = peers * capacity
    half = vocab_shard // 2
    rows = slice_dev * topics
    tail = topics - HEAD
    packed = capacity + tail + tail // 3
    groups = 4
    group = peers // groups
    where = jnp.stack([chip, core]).astype(I32)

    def local(*dims, dtype=F32):
        return pltpu.VMEM(dims, dtype)

    beta = jnp.swapaxes(beta_mean, 1, 2)
    code, doc, count = call(
        functools.partial(place_kernel, peers, capacity, shift, slice_dev),
        [local(peers, capacity)] * 3,
        doc_slice,
        where,
        word_ids,
        word_counts,
        scalars=2,
    )
    top = jnp.max(beta, axis=2)
    mass = jnp.sum(jnp.exp(beta - top[:, :, None]), axis=2)
    stats = jnp.concatenate([top.reshape(1, 1, -1), mass.reshape(1, 1, -1)], axis=2)
    outgoing = jnp.concatenate(
        [code.reshape(peers, 1, capacity), jnp.broadcast_to(stats, (peers, 1, stats.shape[2]))], axis=2
    )

    def exchange(value):
        return lax.all_to_all(value, "doc", split_axis=0, concat_axis=0, tiled=True)

    arrived = exchange(outgoing)
    (coef,) = call(
        functools.partial(coef_kernel, chips),
        [local(topics, NCOEF)],
        where,
        drift_var.reshape(1, topics),
        obs_var.reshape(1, topics),
        scalars=1,
        scratch=[local(NCOEF, 2 * HEAD)],
    )
    asked = arrived[:, 0, :capacity]
    tops = arrived[:, 0, capacity : capacity + rows]
    masses = arrived[:, 0, capacity + rows :]
    highest = jnp.max(tops, axis=0)
    log_norm = highest + jnp.log(jnp.sum(masses * jnp.exp(tops - highest), axis=0))
    log_norm = jnp.pad(log_norm, (0, 4 * HEAD - rows)).reshape(1, -1)
    flat = local(groups, places // groups)
    table, fetched = call(
        functools.partial(fetch_kernel, shift),
        [local(rows, vocab_shard, dtype=BF16), shape((peers, packed, HEAD), BF16)],
        beta.reshape(rows, vocab_shard),
        log_norm,
        asked,
        scratch=[flat],
    )
    asked_late, fetched = lax.optimization_barrier((asked, fetched))
    got = exchange(fetched)
    low, block, mask = call(
        functools.partial(index_kernel, shift, docs),
        [
            local(places, 2 * HEAD, dtype=BF16),
            local(1, places),
            local(peers * docs, places // groups, dtype=BF16),
        ],
        asked_late,
        scratch=[flat],
    )
    got, low, block, mask = lax.optimization_barrier((got, low, block, mask))
    gamma, factors = call(
        estep_kernel,
        [shape((docs, topics), F32), shape((peers, docs + tail // 3 + 8, HEAD), BF16)],
        got,
        doc,
        count,
        word_counts,
        dirichlet.reshape(1, topics),
        scratch=[
            local(places, HEAD, dtype=BF16),
            local(tail, places),
            local(tail, places, dtype=BF16),
            local(1, places),
            local(1, places),
        ],
    )
    factors = exchange(factors)
    send, factor = call(
        functools.partial(send_kernel, docs, capacity),
        [local(rows, half), local(topics, places, dtype=BF16)],
        where,
        factors,
        mask,
        low,
        block,
        table,
        scalars=1,
        scratch=[local(1, places // groups)],
    )
    swap = [(i, i ^ 1) for i in range(time_peers)]
    recv = lax.ppermute(send, "tm", swap)
    (keep,) = call(keep_kernel, [local(rows, half)], where, factor, low, block, table, scalars=1)
    (combined,) = call(
        combine_kernel, [shape((chips, topics, half), BF16)], where, coef, keep, recv, scalars=1
    )
    far = lax.all_to_all(
        combined,
        "tm",
        split_axis=0,
        concat_axis=0,
        tiled=True,
        axis_index_groups=[[2 * i + c for i in range(chips)] for c in range(2)],
    )
    own, other = call(
        edges_kernel, [local(slice_dev, topics, half)] * 2, where, coef, keep, recv, far, scalars=1
    )
    partner = lax.ppermute(other, "tm", swap)
    (means,) = call(
        means_kernel,
        [shape((slice_dev, topics, vocab_shard), F32)],
        where,
        coef,
        keep,
        send,
        own,
        partner,
        scalars=1,
    )
    return jnp.swapaxes(means, 1, 2), gamma


def solution(mesh):
    return jax.shard_map(
        per_device,
        mesh=mesh,
        in_specs=(
            P("tm", "doc", None),
            P(("tm", "doc"), None),
            P(("tm", "doc"), None),
            P(("tm", "doc")),
            P(),
            P(),
            P(),
        ),
        out_specs=(P("tm", "doc", None), P(("tm", "doc"), None)),
        check_vma=False,
    )
```

```python
import functools
import math

import jax
import jax.numpy as jnp
from jax import lax
from jax.experimental import pallas as pl
from jax.experimental.pallas import tpu as pltpu
from jax.sharding import PartitionSpec as P

E_ITERS = 4
PSEUDO = 0.1
PRIOR_VAR = 1.0
LOG_PSEUDO = math.log(PSEUDO)
F32, BF16, I32 = jnp.float32, jnp.bfloat16, jnp.int32
NT = (((1,), (1,)), ((), ()))
TN = (((0,), (0,)), ((), ()))
SMEM = pl.BlockSpec(memory_space=pltpu.SMEM)


def iota(shape, axis):
    return lax.broadcasted_iota(I32, shape, axis)


def mm(a, b):
    return jnp.dot(a, b, preferred_element_type=F32)


def mmg(a, b, dims):
    return lax.dot_general(a, b, dims, preferred_element_type=F32)


VMEM = pl.BlockSpec(memory_space=pltpu.VMEM)


def shape(dims, dtype):
    return jax.ShapeDtypeStruct(dims, dtype)


def call(kernel, outs, *args, scalars=0, far=0, scratch=()):
    near = len(args) - far
    args = (
        args[:scalars]
        + tuple(pltpu.with_memory_space_constraint(a, pltpu.VMEM) for a in args[scalars:near])
        + tuple(pltpu.with_memory_space_constraint(a, pltpu.HBM) for a in args[near:])
    )
    return pl.pallas_call(
        kernel,
        out_shape=outs,
        in_specs=[SMEM] * scalars + [VMEM] * (near - scalars) + [pl.BlockSpec(memory_space=pltpu.HBM)] * far,
        out_specs=[VMEM if getattr(o, "memory_space", None) == pltpu.VMEM else pl.BlockSpec() for o in outs],
        scratch_shapes=scratch,
        compiler_params=pltpu.CompilerParams(vmem_limit_bytes=36 << 20),
    )(*args)


def place_kernel(peers, capacity, shift, per, slice_ref, where_ref, ids_ref, counts_ref, code_ref, doc_ref, count_ref):
    docs, width = ids_ref.shape
    ids = ids_ref[...]
    owner = lax.shift_right_logical(ids, shift)
    word = ids & ((1 << shift) - 1)
    low = (word & 255).astype(F32)
    high = (lax.shift_right_logical(word, 8) + 1).astype(F32)
    counts = counts_ref[...].astype(F32)
    base = (where_ref[0] * 2 + where_ref[1]) * per
    before = (iota((width, width), 0) < iota((width, width), 1)).astype(F32).astype(BF16)
    owners = iota((peers, width), 0)
    ranks = iota((capacity, width), 0).astype(F32)
    hot = [(owners == owner[d : d + 1, :]).astype(F32) for d in range(docs)]
    inside = mm(jnp.concatenate(hot, axis=0).astype(BF16), before)
    start = jnp.zeros((peers, 1), F32)
    left, right = [], []
    for d in range(docs):
        mine = hot[d]
        part = ((slice_ref[d] - base) << (shift - 8)).astype(F32)
        rank = jnp.sum(mine * (inside[d * peers : (d + 1) * peers] + start), axis=0, keepdims=True)
        start = start + jnp.sum(mine, axis=1, keepdims=True)
        right.append((ranks == rank).astype(F32).astype(BF16))
        left.append(
            jnp.concatenate(
                [
                    mine * low[d : d + 1],
                    mine * (high[d : d + 1] + part),
                    mine * float(d),
                    mine * counts[d : d + 1],
                ],
                axis=0,
            ).astype(BF16)
        )
    placed = mmg(jnp.concatenate(left, axis=1), jnp.concatenate(right, axis=1), NT)
    low_p, high_p, doc_p, count_p = (placed[i * peers : (i + 1) * peers] for i in range(4))
    code_ref[...] = doc_p * 8192.0 + high_p * 256.0 + low_p
    doc_ref[...] = jnp.where(high_p > 0.5, doc_p, -1.0)
    count_ref[...] = count_p


HEAD = 128


def at_of(code):
    return (code & 8191) - 256


def word_of(code, shift):
    return at_of(code) & ((1 << shift) - 1)


def part_of(code, shift):
    return lax.shift_right_logical(at_of(code), shift) & 1


def flatten(flat_ref, rows_ref, group):
    capacity = rows_ref.shape[1]
    for s in range(rows_ref.shape[0]):
        g, i = divmod(s, group)
        flat_ref[g : g + 1, i * capacity : (i + 1) * capacity] = rows_ref[s : s + 1, :]


def tiles(count, grid, low, high):
    return [jnp.where(grid == jnp.where(high == float(h), low, -1.0).astype(BF16), 1.0, 0.0).astype(BF16) for h in range(count)]


def columns(source, code, shift):
    rows, words = source.shape[0] // 2, source.shape[1]
    chunk = 256
    grid = iota((256, chunk), 0).astype(F32).astype(BF16)
    out = []
    for c in range(code.shape[1] // chunk):
        mine = code[:, c * chunk : (c + 1) * chunk]
        word = word_of(mine, shift)
        low, high = (word & 255).astype(F32), lax.shift_right_logical(word, 8).astype(F32)
        both = mm(source[...], jnp.concatenate(tiles(words // 256, grid, low, high), axis=0))
        out.append(jnp.where(part_of(mine, shift) == 0, both[:rows], both[rows:]))
    return jnp.concatenate(out, axis=1)


def fetch_kernel(shift, beta_ref, norm_ref, asked_ref, table_ref, out_ref, flat_ref):
    rows, words = beta_ref.shape
    topics = rows // 2
    tail = topics - HEAD
    peers, capacity = asked_ref.shape
    groups = flat_ref.shape[0]
    group = peers // groups
    norm = jnp.transpose(jnp.broadcast_to(norm_ref[...], (8, norm_ref.shape[1])))[:, 0:1]
    step = 40
    for r in range(0, rows, step):
        table_ref[r : r + step, :] = jnp.exp(beta_ref[r : r + step, :] - norm[r : r + step]).astype(BF16)
    flatten(flat_ref, asked_ref, group)
    third = tail // 3
    spare = capacity - HEAD

    def one(g, carry):
        got = columns(table_ref, flat_ref[pl.ds(g, 1), :].astype(I32), shift)
        wide = jnp.transpose(got[:HEAD]).astype(BF16)
        for i in range(group):
            mine = got[HEAD:, i * capacity : (i + 1) * capacity]
            rest = [mine[b * third : (b + 1) * third, HEAD:] for b in range(3)]
            rest.append(jnp.zeros((third, HEAD - 3 * spare), F32))
            out_ref[g * group + i, 0:capacity, :] = wide[i * capacity : (i + 1) * capacity]
            out_ref[g * group + i, capacity : capacity + tail, :] = mine[:, :HEAD].astype(BF16)
            out_ref[g * group + i, capacity + tail :, :] = jnp.concatenate(rest, axis=1).astype(BF16)
        return carry

    lax.fori_loop(0, groups, one, 0)


def index_kernel(shift, docs, asked_ref, low_ref, block_ref, key_ref, flat_ref):
    peers, capacity = asked_ref.shape
    groups, places = flat_ref.shape
    group = peers // groups
    flatten(flat_ref, asked_ref, group)
    lane = iota((1, places), 1)
    chunk = low_ref.shape[1]
    grid = iota((places, chunk), 1).astype(F32).astype(BF16)
    for g in range(groups):
        code = flat_ref[g : g + 1, :].astype(I32)
        key = jnp.where(code == 0, -1, lax.shift_right_logical(code, 13))
        for s in range(1, group):
            key = key + jnp.where(lane >= s * capacity, jnp.where(code == 0, 0, docs), 0)
        at = at_of(code) & ((2 << shift) - 1)
        low = (at & (chunk - 1)).astype(F32)
        key_ref[:, g * places : (g + 1) * places] = key.astype(F32)
        block_ref[:, g * places : (g + 1) * places] = lax.shift_right_logical(at, chunk.bit_length() - 1).astype(F32)
        column = jnp.transpose(jnp.broadcast_to(low, (8, places)))[:, 0:1].astype(BF16)
        low_ref[g * places : (g + 1) * places, :] = jnp.where(grid == column, 1.0, 0.0).astype(BF16)


def digamma(value):
    correction = jnp.zeros_like(value)
    for j in range(6):
        correction = correction + 1.0 / (value + float(j))
    shifted = value + 6.0
    inverse = 1.0 / shifted
    square = inverse * inverse
    series = square * (1.0 / 12.0 - square * (1.0 / 120.0 - square * (1.0 / 252.0)))
    return jnp.log(shifted) - 0.5 * inverse - series - correction


def split(value):
    high = value.astype(BF16)
    return high, (value - high.astype(F32)).astype(BF16)


def estep_kernel(
    got_ref, doc_rows, count_rows, counts_ref, dirichlet_ref, gamma_ref, out_ref, head_ref, wide_ref, tail_ref, doc_ref, count_ref
):
    docs = counts_ref.shape[0]
    topics = dirichlet_ref.shape[1]
    tail = topics - HEAD
    third = tail // 3
    peers, capacity = doc_rows.shape
    spare = capacity - HEAD
    flatten(doc_ref, doc_rows, peers)
    flatten(count_ref, count_rows, peers)
    for s in range(peers):
        at = s * capacity
        head_ref[at : at + capacity, :] = got_ref[s, :capacity, :]
        wide_ref[:, at : at + HEAD] = got_ref[s, capacity : capacity + tail, :].astype(F32)
        left = got_ref[s, capacity + tail :, :].astype(F32)
        for b in range(3):
            wide_ref[b * third : (b + 1) * third, at + HEAD : at + capacity] = left[:, b * spare : (b + 1) * spare]
    tail_ref[...] = wide_ref[...].astype(BF16)
    dirichlet = dirichlet_ref[...]
    total = jnp.sum(counts_ref[...].astype(F32), axis=1, keepdims=True)
    gamma = dirichlet + total / float(topics)
    doc = doc_ref[...]
    mask = iota((docs, doc.shape[1]), 0) == doc.astype(I32)
    for step in range(E_ITERS):
        theta = jnp.exp(digamma(gamma) - digamma(jnp.sum(gamma, axis=1, keepdims=True)))
        both = jnp.concatenate(split(theta), axis=0)
        norm = mmg(both[:, :HEAD], head_ref[...], NT) + mm(both[:, HEAD:], tail_ref[...])
        norm = norm[:docs] + norm[docs:]
        norm = jnp.sum(jnp.where(mask, norm, 0.0), axis=0, keepdims=True)
        ratio = jnp.where(doc >= 0.0, count_ref[...] / norm, 0.0)
        high, low = split(ratio)
        high, low = high.astype(F32), low.astype(F32)
        spread = jnp.concatenate([jnp.where(mask, high, 0.0), jnp.where(mask, low, 0.0)], axis=0).astype(BF16)
        part = jnp.concatenate([mm(spread, head_ref[...]), mmg(spread, tail_ref[...], NT)], axis=1)
        gamma = dirichlet + theta * (part[:docs] + part[docs:])
    gamma_ref[...] = gamma
    turned = jnp.transpose(jnp.concatenate([theta[:, HEAD:], jnp.zeros((docs, 2 * HEAD - topics), F32)], axis=1))
    turned = [turned[b * third : (b + 1) * third, :] for b in range(3)]
    turned.append(jnp.zeros((third, HEAD - 3 * docs), F32))
    common = jnp.concatenate([theta[:, :HEAD], jnp.concatenate(turned, axis=1)], axis=0).astype(BF16)
    pad = jnp.zeros((1, HEAD - spare), F32)
    blank = jnp.zeros((4, HEAD), F32)
    for s in range(peers):
        at = s * capacity
        rows = []
        for piece in (high, low):
            rows.append(piece[:, at : at + HEAD])
            rows.append(jnp.concatenate([piece[:, at + HEAD : at + capacity], pad], axis=1))
        out_ref[s, 0 : docs + third, :] = common
        out_ref[s, docs + third : docs + third + 8, :] = jnp.concatenate(rows + [blank], axis=0).astype(BF16)


def factor_of(docs, capacity, factor_in, key_ref, ratio_ref, out_ref):
    peers = factor_in.shape[0]
    topics, places = out_ref.shape[0], ratio_ref.shape[1]
    group = places // capacity
    grid = iota((group * docs, places), 0).astype(F32).astype(BF16)
    third = (topics - HEAD) // 3
    spare = capacity - HEAD
    for g in range(peers // group):
        turned = []
        for i in range(group):
            block = factor_in[g * group + i, docs : docs + third + 8, :].astype(F32)
            turned.append(jnp.concatenate([block[:third, b * docs : (b + 1) * docs] for b in range(3)], axis=0))
            ratio = block[third : third + 2] + block[third + 2 : third + 4]
            ratio_ref[0:1, i * capacity : i * capacity + HEAD] = ratio[0:1]
            ratio_ref[0:1, i * capacity + HEAD : (i + 1) * capacity] = ratio[1:2, :spare]
        at = slice(g * places, (g + 1) * places)
        mask = jnp.where(grid == key_ref[:, at].astype(BF16), 1.0, 0.0).astype(BF16)
        top = factor_in[g * group : (g + 1) * group, :docs, :].reshape(group * docs, HEAD)
        bottom = jnp.concatenate(turned, axis=1).astype(BF16)
        ratio = ratio_ref[...]
        out_ref[:HEAD, at] = (mmg(top, mask, TN) * ratio).astype(BF16)
        out_ref[HEAD:, at] = (mm(bottom, mask) * ratio).astype(BF16)


def half_stats(half, factor_ref, low_ref, block_ref, table_ref, out_ref):
    topics = factor_ref.shape[0]
    parts = table_ref.shape[0] // topics
    chunk = low_ref.shape[1]
    blocks = table_ref.shape[1] // chunk
    block = block_ref[...]
    for t in range(parts):
        for q in range(blocks // 2):
            h = half * (blocks // 2) + q
            here = jnp.where(block == (t * blocks + h).astype(F32), 1.0, 0.0).astype(BF16)
            total = mm(factor_ref[...] * here, low_ref[...])
            words = pl.ds(pl.multiple_of(h * chunk, chunk), chunk)
            table = table_ref[t * topics : (t + 1) * topics, words].astype(F32)
            out_ref[t * topics : (t + 1) * topics, q * chunk : (q + 1) * chunk] = jnp.log(
                1.0 + (1.0 / PSEUDO) * (table * total)
            )


def send_kernel(
    docs,
    capacity,
    where_ref,
    factor_in,
    key_ref,
    low_ref,
    block_ref,
    table_hbm,
    out_ref,
    factor_ref,
    table_ref,
    ratio_ref,
    sem,
):
    load = pltpu.make_async_copy(table_hbm, table_ref, sem)
    load.start()
    factor_of(docs, capacity, factor_in, key_ref, ratio_ref, factor_ref)
    load.wait()
    half_stats(1 - where_ref[1], factor_ref, low_ref, block_ref, table_ref, out_ref)


def keep_kernel(where_ref, factor_ref, low_ref, block_ref, table_ref, out_ref):
    half_stats(where_ref[1], factor_ref, low_ref, block_ref, table_ref, out_ref)


G0, S0, H0, B0, PHI0, QK, KNEXT, PHI, WF0, WQ0, NCOEF = 0, 4, 8, 12, 16, 20, 21, 22, 23, 27, 32


def coef_kernel(chips, chip_ref, drift_ref, obs_ref, out_ref, rows_ref):
    per = 4
    length = chips * per
    drift, obs = drift_ref[...], obs_ref[...]
    one, zero = jnp.ones_like(drift), jnp.zeros_like(drift)
    var = one * PRIOR_VAR
    gain, smooth = [], []
    for t in range(length):
        pred = var + drift
        now = pred / (pred + obs)
        var = (1.0 - now) * pred
        gain.append(now)
        smooth.append(var / (var + drift) if t < length - 1 else zero)
    level, forward = zero, []
    for t in range(length):
        level = (1.0 - gain[t]) * level + gain[t]
        forward.append(level)
    ones_smoothed = [None] * length
    level = zero
    for t in reversed(range(length)):
        level = (1.0 - smooth[t]) * forward[t] + smooth[t] * level
        ones_smoothed[t] = level
    beta, phi, sigma, kappa = [], [], [], []
    for c in range(chips):
        run, back, k = one, one, zero
        for t in range(c * per, (c + 1) * per):
            run = run * (1.0 - gain[t])
            phi.append(run)
            beta.append(back * (1.0 - smooth[t]))
            k = k + beta[t] * run
            back = back * smooth[t]
        sigma.append(back)
        kappa.append(k)
    total = [phi[c * per + per - 1] for c in range(chips)]
    lead = [zero] * (chips + 1)
    for c in reversed(range(chips)):
        lead[c] = kappa[c] + sigma[c] * lead[c + 1] * total[c]
    chip = chip_ref[0]
    for c in range(chips):
        rows = [None] * NCOEF
        for u in range(per):
            t = c * per + u
            rows[G0 + u], rows[S0 + u], rows[H0 + u] = gain[t], smooth[t], ones_smoothed[t] * LOG_PSEUDO
            rows[B0 + u], rows[PHI0 + u] = beta[t], phi[t]
        rows[QK], rows[KNEXT], rows[PHI] = sigma[c] * lead[c + 1], lead[c + 1], total[c]
        for j in range(chips):
            behind, ahead = zero, zero
            if j < c:
                behind = one
                for m in range(j + 1, c):
                    behind = behind * total[m]
            if j > c:
                ahead = one
                for m in range(c + 1, j):
                    ahead = ahead * sigma[m]
            rows[WF0 + j], rows[WQ0 + j] = behind, ahead

        @pl.when(chip == c)
        def _():
            for r in range(NCOEF):
                rows_ref[r : r + 1, : drift.shape[1]] = zero if rows[r] is None else rows[r]

    out_ref[...] = jnp.transpose(rows_ref[...])[: out_ref.shape[0]]


def local_filter(coef, values):
    out, level = [], None
    for u in range(4):
        gain = coef[:, G0 + u : G0 + u + 1]
        level = gain * values[u] if level is None else (1.0 - gain) * level + gain * values[u]
        out.append(level)
    return out


def four(first, keep_ref, recv_ref, topics, at):
    own = [keep_ref[pl.ds(u * topics + at, 8), :] for u in range(2)]
    other = [recv_ref[pl.ds(u * topics + at, 8), :] for u in range(2)]
    return [jnp.where(first, own[u], other[u]) for u in range(2)] + [
        jnp.where(first, other[u], own[u]) for u in range(2)
    ]


def combine_kernel(where_ref, coef_ref, keep_ref, recv_ref, out_ref):
    chips, topics, _ = out_ref.shape
    first, chip = where_ref[1] == 0, where_ref[0]

    def block(i, carry):
        at = pl.multiple_of(i * 8, 8)
        coef = coef_ref[pl.ds(at, 8), :]
        local = local_filter(coef, four(first, keep_ref, recv_ref, topics, at))
        back = coef[:, QK : QK + 1] * local[3]
        for u in range(4):
            back = back + coef[:, B0 + u : B0 + u + 1] * local[u]
        for j in range(chips):
            out_ref[j, pl.ds(at, 8), :] = jnp.where(j > chip, local[3], back).astype(BF16)
        return carry

    lax.fori_loop(0, topics // 8, block, 0, unroll=5)


def edges_kernel(where_ref, coef_ref, keep_ref, recv_ref, far_ref, own_ref, other_ref):
    chips, topics, _ = far_ref.shape
    first = where_ref[1] == 0

    def block(i, carry):
        at = pl.multiple_of(i * 8, 8)
        coef = coef_ref[pl.ds(at, 8), :]

        def take(r):
            return coef[:, r : r + 1]

        local = local_filter(coef, four(first, keep_ref, recv_ref, topics, at))
        entering = jnp.zeros_like(local[0])
        ahead = jnp.zeros_like(local[0])
        for j in range(chips):
            far = far_ref[j, pl.ds(at, 8), :].astype(F32)
            entering = entering + take(WF0 + j) * far
            ahead = ahead + take(WQ0 + j) * far
        after = ahead + take(KNEXT) * (local[3] + take(PHI) * entering)
        middle = after
        for u in (3, 2):
            weight = take(S0 + u)
            middle = (1.0 - weight) * (local[u] + take(PHI0 + u) * entering) + weight * middle
        half = local[1] + take(PHI0 + 1) * entering
        own_ref[0, pl.ds(at, 8), :] = jnp.where(first, entering, half)
        own_ref[1, pl.ds(at, 8), :] = jnp.where(first, middle, after)
        other_ref[0, pl.ds(at, 8), :] = jnp.where(first, half, entering).astype(BF16)
        other_ref[1, pl.ds(at, 8), :] = jnp.where(first, after, middle).astype(BF16)
        return carry

    lax.fori_loop(0, topics // 8, block, 0, unroll=5)


def means_kernel(where_ref, coef_ref, keep_ref, send_ref, own_ref, other_ref, out_ref):
    _, topics, words = out_ref.shape
    half = words // 2
    first = where_ref[1] == 0

    def block(i, carry):
        at = pl.multiple_of(i * 8, 8)
        coef = coef_ref[pl.ds(at, 8), :]

        def take(r):
            return jnp.where(first, coef[:, r : r + 1], coef[:, r + 2 : r + 3])

        gain, weight, level = ([take(r + u) for u in range(2)] for r in (G0, S0, H0))
        sides = []
        for value_ref, edge_ref in ((keep_ref, own_ref), (send_ref, other_ref)):
            values = [value_ref[pl.ds(u * topics + at, 8), :] for u in range(2)]
            early = (1.0 - gain[0]) * edge_ref[0, pl.ds(at, 8), :].astype(F32) + gain[0] * values[0]
            late = (1.0 - gain[1]) * early + gain[1] * values[1]
            late = (1.0 - weight[1]) * late + weight[1] * edge_ref[1, pl.ds(at, 8), :].astype(F32)
            early = (1.0 - weight[0]) * early + weight[0] * late
            sides.append((early + level[0], late + level[1]))
        for u in range(2):
            out_ref[u, pl.ds(at, 8), :half] = jnp.where(first, sides[0][u], sides[1][u])
            out_ref[u, pl.ds(at, 8), half:] = jnp.where(first, sides[1][u], sides[0][u])
        return carry

    lax.fori_loop(0, topics // 8, block, 0, unroll=5)


def per_device(beta_mean, word_ids, word_counts, doc_slice, dirichlet, drift_var, obs_var):
    slice_dev, vocab_shard, topics = beta_mean.shape
    docs, width = word_ids.shape
    peers = lax.axis_size("doc")
    time_peers = lax.axis_size("tm")
    here = lax.axis_index("tm")
    chip, core = here // 2, here % 2
    chips = time_peers // 2
    shift = vocab_shard.bit_length() - 1
    slots = docs * width
    capacity = slots * 5 // (4 * peers)
    places = peers * capacity
    half = vocab_shard // 2
    rows = slice_dev * topics
    tail = topics - HEAD
    packed = capacity + tail + tail // 3
    groups = 4
    group = peers // groups
    where = jnp.stack([chip, core]).astype(I32)

    def local(*dims, dtype=F32):
        return pltpu.VMEM(dims, dtype)

    beta = jnp.swapaxes(beta_mean, 1, 2)
    code, doc, count = call(
        functools.partial(place_kernel, peers, capacity, shift, slice_dev),
        [local(peers, capacity)] * 3,
        doc_slice,
        where,
        word_ids,
        word_counts,
        scalars=2,
    )
    top = jnp.max(beta, axis=2)
    mass = jnp.sum(jnp.exp(beta - top[:, :, None]), axis=2)
    stats = jnp.concatenate([top.reshape(1, 1, -1), mass.reshape(1, 1, -1)], axis=2)
    outgoing = jnp.concatenate(
        [code.reshape(peers, 1, capacity), jnp.broadcast_to(stats, (peers, 1, stats.shape[2]))], axis=2
    )

    def exchange(value):
        return lax.all_to_all(value, "doc", split_axis=0, concat_axis=0, tiled=True)

    arrived = exchange(outgoing)
    (coef,) = call(
        functools.partial(coef_kernel, chips),
        [local(topics, NCOEF)],
        where,
        drift_var.reshape(1, topics),
        obs_var.reshape(1, topics),
        scalars=1,
        scratch=[local(NCOEF, 2 * HEAD)],
    )
    asked = arrived[:, 0, :capacity]
    tops = arrived[:, 0, capacity : capacity + rows]
    masses = arrived[:, 0, capacity + rows :]
    highest = jnp.max(tops, axis=0)
    log_norm = highest + jnp.log(jnp.sum(masses * jnp.exp(tops - highest), axis=0))
    log_norm = jnp.pad(log_norm, (0, 4 * HEAD - rows)).reshape(1, -1)
    flat = local(groups, places // groups)
    table, fetched = call(
        functools.partial(fetch_kernel, shift),
        [pltpu.HBM((rows, vocab_shard), BF16), pltpu.HBM((peers, packed, HEAD), BF16)],
        beta.reshape(rows, vocab_shard),
        log_norm,
        asked,
        scratch=[flat],
    )
    got = exchange(fetched)
    gamma, factors = call(
        estep_kernel,
        [shape((docs, topics), F32), shape((peers, docs + tail // 3 + 8, HEAD), BF16)],
        got,
        doc,
        count,
        word_counts,
        dirichlet.reshape(1, topics),
        scratch=[
            local(places, HEAD, dtype=BF16),
            local(tail, places),
            local(tail, places, dtype=BF16),
            local(1, places),
            local(1, places),
        ],
    )
    asked_late, factors = lax.optimization_barrier((asked, factors))
    factors = exchange(factors)
    low, block, key = call(
        functools.partial(index_kernel, shift, docs),
        [local(places, 2 * HEAD, dtype=BF16), local(1, places), local(1, places)],
        asked_late,
        scratch=[flat],
    )
    factors, low, block, key = lax.optimization_barrier((factors, low, block, key))
    send, factor, table = call(
        functools.partial(send_kernel, docs, capacity),
        [local(rows, half), local(topics, places, dtype=BF16), local(rows, vocab_shard, dtype=BF16)],
        where,
        factors,
        key,
        low,
        block,
        table,
        scalars=1,
        far=1,
        scratch=[local(1, places // groups), pltpu.SemaphoreType.DMA(())],
    )
    swap = [(i, i ^ 1) for i in range(time_peers)]
    recv = lax.ppermute(send, "tm", swap)
    (keep,) = call(keep_kernel, [local(rows, half)], where, factor, low, block, table, scalars=1)
    (combined,) = call(
        combine_kernel, [shape((chips, topics, half), BF16)], where, coef, keep, recv, scalars=1
    )
    far = lax.all_to_all(
        combined,
        "tm",
        split_axis=0,
        concat_axis=0,
        tiled=True,
        axis_index_groups=[[2 * i + c for i in range(chips)] for c in range(2)],
    )
    own, other = call(
        edges_kernel,
        [local(slice_dev, topics, half), local(slice_dev, topics, half, dtype=BF16)],
        where,
        coef,
        keep,
        recv,
        far,
        scalars=1,
    )
    partner = lax.ppermute(other, "tm", swap)
    (means,) = call(
        means_kernel,
        [shape((slice_dev, topics, vocab_shard), F32)],
        where,
        coef,
        keep,
        send,
        own,
        partner,
        scalars=1,
    )
    return jnp.swapaxes(means, 1, 2), gamma


def solution(mesh):
    return jax.shard_map(
        per_device,
        mesh=mesh,
        in_specs=(
            P("tm", "doc", None),
            P(("tm", "doc"), None),
            P(("tm", "doc"), None),
            P(("tm", "doc")),
            P(),
            P(),
            P(),
        ),
        out_specs=(P("tm", "doc", None), P(("tm", "doc"), None)),
        check_vma=False,
    )
```

```python
import functools
import math

import jax
import jax.numpy as jnp
from jax import lax
from jax.experimental import pallas as pl
from jax.experimental.pallas import tpu as pltpu
from jax.sharding import PartitionSpec as P

E_ITERS = 4
PSEUDO = 0.1
PRIOR_VAR = 1.0
LOG_PSEUDO = math.log(PSEUDO)
F32, BF16, I32 = jnp.float32, jnp.bfloat16, jnp.int32
NT = (((1,), (1,)), ((), ()))
TN = (((0,), (0,)), ((), ()))
SMEM = pl.BlockSpec(memory_space=pltpu.SMEM)


def iota(shape, axis):
    return lax.broadcasted_iota(I32, shape, axis)


def hot(true):
    return true.astype(F32).astype(BF16)


def mm(a, b):
    return jnp.dot(a, b, preferred_element_type=F32)


def mmg(a, b, dims):
    return lax.dot_general(a, b, dims, preferred_element_type=F32)


VMEM = pl.BlockSpec(memory_space=pltpu.VMEM)


def shape(dims, dtype):
    return jax.ShapeDtypeStruct(dims, dtype)


def call(kernel, outs, *args, scalars=0, far=0, scratch=()):
    near = len(args) - far
    args = (
        args[:scalars]
        + tuple(pltpu.with_memory_space_constraint(a, pltpu.VMEM) for a in args[scalars:near])
        + tuple(pltpu.with_memory_space_constraint(a, pltpu.HBM) for a in args[near:])
    )
    return pl.pallas_call(
        kernel,
        out_shape=outs,
        in_specs=[SMEM] * scalars + [VMEM] * (near - scalars) + [pl.BlockSpec(memory_space=pltpu.HBM)] * far,
        out_specs=[VMEM if getattr(o, "memory_space", None) == pltpu.VMEM else pl.BlockSpec() for o in outs],
        scratch_shapes=scratch,
        compiler_params=pltpu.CompilerParams(vmem_limit_bytes=36 << 20),
    )(*args)


def place_kernel(peers, capacity, shift, per, slice_ref, where_ref, ids_ref, counts_ref, code_ref, doc_ref, count_ref):
    docs, width = ids_ref.shape
    ids = ids_ref[...]
    owner = lax.shift_right_logical(ids, shift)
    word = ids & ((1 << shift) - 1)
    low = (word & 255).astype(F32)
    high = (lax.shift_right_logical(word, 8) + 1).astype(F32)
    counts = counts_ref[...].astype(F32)
    base = (where_ref[0] * 2 + where_ref[1]) * per
    before = (iota((width, width), 0) < iota((width, width), 1)).astype(F32).astype(BF16)
    owners = iota((peers, width), 0)
    ranks = iota((capacity, width), 0).astype(F32)
    hot = [(owners == owner[d : d + 1, :]).astype(F32) for d in range(docs)]
    inside = mm(jnp.concatenate(hot, axis=0).astype(BF16), before)
    start = jnp.zeros((peers, 1), F32)
    left, right = [], []
    for d in range(docs):
        mine = hot[d]
        part = ((slice_ref[d] - base) << (shift - 8)).astype(F32)
        rank = jnp.sum(mine * (inside[d * peers : (d + 1) * peers] + start), axis=0, keepdims=True)
        start = start + jnp.sum(mine, axis=1, keepdims=True)
        right.append((ranks == rank).astype(F32).astype(BF16))
        left.append(
            jnp.concatenate(
                [
                    mine * low[d : d + 1],
                    mine * (high[d : d + 1] + part),
                    mine * float(d),
                    mine * counts[d : d + 1],
                ],
                axis=0,
            ).astype(BF16)
        )
    placed = mmg(jnp.concatenate(left, axis=1), jnp.concatenate(right, axis=1), NT)
    low_p, high_p, doc_p, count_p = (placed[i * peers : (i + 1) * peers] for i in range(4))
    code_ref[...] = doc_p * 8192.0 + high_p * 256.0 + low_p
    doc_ref[...] = jnp.where(high_p > 0.5, doc_p, -1.0)
    count_ref[...] = count_p


HEAD = 128


def at_of(code):
    return (code & 8191) - 256


def word_of(code, shift):
    return at_of(code) & ((1 << shift) - 1)


def part_of(code, shift):
    return lax.shift_right_logical(at_of(code), shift) & 1


def flatten(flat_ref, rows_ref, group):
    capacity = rows_ref.shape[1]
    for s in range(rows_ref.shape[0]):
        g, i = divmod(s, group)
        flat_ref[g : g + 1, i * capacity : (i + 1) * capacity] = rows_ref[s : s + 1, :]


def tiles(count, grid, low, high):
    return [hot(grid == jnp.where(high == float(h), low, -1.0)) for h in range(count)]


def columns(source, code, shift):
    rows, words = source.shape[0] // 2, source.shape[1]
    chunk = 256
    grid = iota((256, chunk), 0).astype(F32)
    out = []
    for c in range(code.shape[1] // chunk):
        mine = code[:, c * chunk : (c + 1) * chunk]
        word = word_of(mine, shift)
        low, high = (word & 255).astype(F32), lax.shift_right_logical(word, 8).astype(F32)
        both = mm(source[...], jnp.concatenate(tiles(words // 256, grid, low, high), axis=0))
        out.append(jnp.where(part_of(mine, shift) == 0, both[:rows], both[rows:]))
    return jnp.concatenate(out, axis=1)


def fetch_kernel(shift, beta_ref, norm_ref, asked_ref, table_ref, out_ref, flat_ref):
    rows, words = beta_ref.shape
    topics = rows // 2
    tail = topics - HEAD
    peers, capacity = asked_ref.shape
    groups = flat_ref.shape[0]
    group = peers // groups
    norm = jnp.transpose(jnp.broadcast_to(norm_ref[...], (8, norm_ref.shape[1])))[:, 0:1]
    step = 40
    for r in range(0, rows, step):
        table_ref[r : r + step, :] = jnp.exp(beta_ref[r : r + step, :] - norm[r : r + step]).astype(BF16)
    flatten(flat_ref, asked_ref, group)
    third = tail // 3
    spare = capacity - HEAD

    def one(g, carry):
        got = columns(table_ref, flat_ref[pl.ds(g, 1), :].astype(I32), shift)
        wide = jnp.transpose(got[:HEAD]).astype(BF16)
        for i in range(group):
            mine = got[HEAD:, i * capacity : (i + 1) * capacity]
            rest = [mine[b * third : (b + 1) * third, HEAD:] for b in range(3)]
            rest.append(jnp.zeros((third, HEAD - 3 * spare), F32))
            out_ref[g * group + i, 0:capacity, :] = wide[i * capacity : (i + 1) * capacity]
            out_ref[g * group + i, capacity : capacity + tail, :] = mine[:, :HEAD].astype(BF16)
            out_ref[g * group + i, capacity + tail :, :] = jnp.concatenate(rest, axis=1).astype(BF16)
        return carry

    lax.fori_loop(0, groups, one, 0)


def index_kernel(shift, docs, pack, asked_ref, low_ref, block_ref, key_ref, flat_ref):
    peers, capacity = asked_ref.shape
    groups, places = flat_ref.shape
    group = peers // groups
    flatten(flat_ref, asked_ref, group)
    lane = iota((1, places), 1)
    chunk = low_ref.shape[1]
    grid = iota((places, chunk), 1).astype(F32)
    for g in range(groups):
        code = flat_ref[g : g + 1, :].astype(I32)
        key = jnp.where(code == 0, -1, lax.shift_right_logical(code, 13))
        for s in range(1, group):
            more = docs if s % pack else (1 - pack) * docs
            key = key + jnp.where(lane >= s * capacity, jnp.where(code == 0, 0, more), 0)
        at = at_of(code) & ((2 << shift) - 1)
        low = (at & (chunk - 1)).astype(F32)
        key_ref[:, g * places : (g + 1) * places] = key.astype(F32)
        block_ref[:, g * places : (g + 1) * places] = lax.shift_right_logical(at, chunk.bit_length() - 1).astype(F32)
        column = jnp.transpose(jnp.broadcast_to(low, (8, places)))[:, 0:1]
        low_ref[g * places : (g + 1) * places, :] = hot(grid == column)


def digamma(value):
    correction = jnp.zeros_like(value)
    for j in range(6):
        correction = correction + 1.0 / (value + float(j))
    shifted = value + 6.0
    inverse = 1.0 / shifted
    square = inverse * inverse
    series = square * (1.0 / 12.0 - square * (1.0 / 120.0 - square * (1.0 / 252.0)))
    return jnp.log(shifted) - 0.5 * inverse - series - correction


def split(value):
    high = value.astype(BF16)
    return high, (value - high.astype(F32)).astype(BF16)


def estep_kernel(
    got_ref, doc_rows, count_rows, counts_ref, dirichlet_ref, gamma_ref, out_ref, head_ref, wide_ref, tail_ref, doc_ref, count_ref
):
    docs = counts_ref.shape[0]
    topics = dirichlet_ref.shape[1]
    tail = topics - HEAD
    third = tail // 3
    peers, capacity = doc_rows.shape
    spare = capacity - HEAD
    flatten(doc_ref, doc_rows, peers)
    flatten(count_ref, count_rows, peers)
    for s in range(peers):
        at = s * capacity
        head_ref[at : at + capacity, :] = got_ref[s, :capacity, :]
        wide_ref[:, at : at + HEAD] = got_ref[s, capacity : capacity + tail, :].astype(F32)
        left = got_ref[s, capacity + tail :, :].astype(F32)
        for b in range(3):
            wide_ref[b * third : (b + 1) * third, at + HEAD : at + capacity] = left[:, b * spare : (b + 1) * spare]
    tail_ref[...] = wide_ref[...].astype(BF16)
    dirichlet = dirichlet_ref[...]
    total = jnp.sum(counts_ref[...].astype(F32), axis=1, keepdims=True)
    gamma = dirichlet + total / float(topics)
    doc = doc_ref[...]
    mask = iota((docs, doc.shape[1]), 0) == doc.astype(I32)
    for step in range(E_ITERS):
        theta = jnp.exp(digamma(gamma) - digamma(jnp.sum(gamma, axis=1, keepdims=True)))
        both = jnp.concatenate(split(theta), axis=0)
        norm = mmg(both[:, :HEAD], head_ref[...], NT) + mm(both[:, HEAD:], tail_ref[...])
        norm = norm[:docs] + norm[docs:]
        norm = jnp.sum(jnp.where(mask, norm, 0.0), axis=0, keepdims=True)
        ratio = jnp.where(doc >= 0.0, count_ref[...] / norm, 0.0)
        high, low = split(ratio)
        high, low = high.astype(F32), low.astype(F32)
        spread = jnp.concatenate([jnp.where(mask, high, 0.0), jnp.where(mask, low, 0.0)], axis=0).astype(BF16)
        part = jnp.concatenate([mm(spread, head_ref[...]), mmg(spread, tail_ref[...], NT)], axis=1)
        gamma = dirichlet + theta * (part[:docs] + part[docs:])
    gamma_ref[...] = gamma
    turned = jnp.transpose(jnp.concatenate([theta[:, HEAD:], jnp.zeros((docs, 2 * HEAD - topics), F32)], axis=1))
    turned = [turned[b * third : (b + 1) * third, :] for b in range(3)]
    turned.append(jnp.zeros((third, HEAD - 3 * docs), F32))
    common = jnp.concatenate([theta[:, :HEAD], jnp.concatenate(turned, axis=1)], axis=0).astype(BF16)
    pad = jnp.zeros((1, HEAD - spare), F32)
    blank = jnp.zeros((4, HEAD), F32)
    for s in range(peers):
        at = s * capacity
        rows = []
        for piece in (high, low):
            rows.append(piece[:, at : at + HEAD])
            rows.append(jnp.concatenate([piece[:, at + HEAD : at + capacity], pad], axis=1))
        out_ref[s, 0 : docs + third, :] = common
        out_ref[s, docs + third : docs + third + 8, :] = jnp.concatenate(rows + [blank], axis=0).astype(BF16)


def factor_of(docs, capacity, factor_in, key_ref, ratio_ref, out_ref):
    peers = factor_in.shape[0]
    topics, places = out_ref.shape[0], ratio_ref.shape[1]
    group = places // capacity
    grid = iota((group * docs, places), 0)
    third = (topics - HEAD) // 3
    spare = capacity - HEAD
    for g in range(peers // group):
        turned = []
        for i in range(group):
            block = factor_in[g * group + i, docs : docs + third + 8, :].astype(F32)
            turned.append(jnp.concatenate([block[:third, b * docs : (b + 1) * docs] for b in range(3)], axis=0))
            ratio = block[third : third + 2] + block[third + 2 : third + 4]
            ratio_ref[0:1, i * capacity : i * capacity + HEAD] = ratio[0:1]
            ratio_ref[0:1, i * capacity + HEAD : (i + 1) * capacity] = ratio[1:2, :spare]
        at = slice(g * places, (g + 1) * places)
        mask = hot(grid == key_ref[:, at].astype(I32))
        top = factor_in[g * group : (g + 1) * group, :docs, :].reshape(group * docs, HEAD)
        bottom = jnp.concatenate(turned, axis=1).astype(BF16)
        ratio = ratio_ref[...]
        out_ref[:HEAD, at] = (mmg(top, mask, TN) * ratio).astype(BF16)
        out_ref[HEAD:, at] = (mm(bottom, mask) * ratio).astype(BF16)


def half_stats(half, factor_ref, low_ref, block_ref, table_ref, out_ref):
    topics = factor_ref.shape[0]
    parts = table_ref.shape[0] // topics
    chunk = low_ref.shape[1]
    blocks = table_ref.shape[1] // chunk
    block = block_ref[...]
    for t in range(parts):
        for q in range(blocks // 2):
            h = half * (blocks // 2) + q
            here = jnp.where(block == (t * blocks + h).astype(F32), 1.0, 0.0).astype(BF16)
            total = mm(factor_ref[...] * here, low_ref[...])
            words = pl.ds(pl.multiple_of(h * chunk, chunk), chunk)
            table = table_ref[t * topics : (t + 1) * topics, words].astype(F32)
            out_ref[t * topics : (t + 1) * topics, q * chunk : (q + 1) * chunk] = jnp.log(
                1.0 + (1.0 / PSEUDO) * (table * total)
            )


def send_kernel(
    docs,
    capacity,
    where_ref,
    factor_in,
    key_ref,
    low_ref,
    block_ref,
    table_hbm,
    out_ref,
    factor_ref,
    table_ref,
    ratio_ref,
    sem,
):
    load = pltpu.make_async_copy(table_hbm, table_ref, sem)
    load.start()
    factor_of(docs, capacity, factor_in, key_ref, ratio_ref, factor_ref)
    load.wait()
    half_stats(1 - where_ref[1], factor_ref, low_ref, block_ref, table_ref, out_ref)


def keep_kernel(where_ref, factor_ref, low_ref, block_ref, table_ref, out_ref):
    half_stats(where_ref[1], factor_ref, low_ref, block_ref, table_ref, out_ref)


G0, S0, H0, B0, PHI0, QK, KNEXT, PHI, WF0, WQ0, NCOEF = 0, 4, 8, 12, 16, 20, 21, 22, 23, 27, 32


def coef_kernel(chips, chip_ref, drift_ref, obs_ref, out_ref, rows_ref):
    per = 4
    length = chips * per
    drift, obs = drift_ref[...], obs_ref[...]
    one, zero = jnp.ones_like(drift), jnp.zeros_like(drift)
    var = one * PRIOR_VAR
    gain, smooth = [], []
    for t in range(length):
        pred = var + drift
        now = pred / (pred + obs)
        var = (1.0 - now) * pred
        gain.append(now)
        smooth.append(var / (var + drift) if t < length - 1 else zero)
    level, forward = zero, []
    for t in range(length):
        level = (1.0 - gain[t]) * level + gain[t]
        forward.append(level)
    ones_smoothed = [None] * length
    level = zero
    for t in reversed(range(length)):
        level = (1.0 - smooth[t]) * forward[t] + smooth[t] * level
        ones_smoothed[t] = level
    beta, phi, sigma, kappa = [], [], [], []
    for c in range(chips):
        run, back, k = one, one, zero
        for t in range(c * per, (c + 1) * per):
            run = run * (1.0 - gain[t])
            phi.append(run)
            beta.append(back * (1.0 - smooth[t]))
            k = k + beta[t] * run
            back = back * smooth[t]
        sigma.append(back)
        kappa.append(k)
    total = [phi[c * per + per - 1] for c in range(chips)]
    lead = [zero] * (chips + 1)
    for c in reversed(range(chips)):
        lead[c] = kappa[c] + sigma[c] * lead[c + 1] * total[c]
    chip = chip_ref[0]
    for c in range(chips):
        rows = [None] * NCOEF
        for u in range(per):
            t = c * per + u
            rows[G0 + u], rows[S0 + u], rows[H0 + u] = gain[t], smooth[t], ones_smoothed[t] * LOG_PSEUDO
            rows[B0 + u], rows[PHI0 + u] = beta[t], phi[t]
        rows[QK], rows[KNEXT], rows[PHI] = sigma[c] * lead[c + 1], lead[c + 1], total[c]
        for j in range(chips):
            behind, ahead = zero, zero
            if j < c:
                behind = one
                for m in range(j + 1, c):
                    behind = behind * total[m]
            if j > c:
                ahead = one
                for m in range(c + 1, j):
                    ahead = ahead * sigma[m]
            rows[WF0 + j], rows[WQ0 + j] = behind, ahead

        @pl.when(chip == c)
        def _():
            for r in range(NCOEF):
                rows_ref[r : r + 1, : drift.shape[1]] = zero if rows[r] is None else rows[r]

    out_ref[...] = jnp.transpose(rows_ref[...])[: out_ref.shape[0]]


def local_filter(coef, values):
    out, level = [], None
    for u in range(4):
        gain = coef[:, G0 + u : G0 + u + 1]
        level = gain * values[u] if level is None else (1.0 - gain) * level + gain * values[u]
        out.append(level)
    return out


def four(first, keep_ref, recv_ref, topics, at):
    own = [keep_ref[pl.ds(u * topics + at, 8), :] for u in range(2)]
    other = [recv_ref[pl.ds(u * topics + at, 8), :] for u in range(2)]
    return [jnp.where(first, own[u], other[u]) for u in range(2)] + [
        jnp.where(first, other[u], own[u]) for u in range(2)
    ]


def combine_kernel(where_ref, coef_ref, keep_ref, recv_ref, out_ref):
    chips, topics, _ = out_ref.shape
    first, chip = where_ref[1] == 0, where_ref[0]

    def block(i, carry):
        at = pl.multiple_of(i * 8, 8)
        coef = coef_ref[pl.ds(at, 8), :]
        local = local_filter(coef, four(first, keep_ref, recv_ref, topics, at))
        back = coef[:, QK : QK + 1] * local[3]
        for u in range(4):
            back = back + coef[:, B0 + u : B0 + u + 1] * local[u]
        for j in range(chips):
            out_ref[j, pl.ds(at, 8), :] = jnp.where(j > chip, local[3], back).astype(BF16)
        return carry

    lax.fori_loop(0, topics // 8, block, 0, unroll=5)


def edges_kernel(where_ref, coef_ref, keep_ref, recv_ref, far_ref, own_ref, other_ref):
    chips, topics, _ = far_ref.shape
    first = where_ref[1] == 0

    def block(i, carry):
        at = pl.multiple_of(i * 8, 8)
        coef = coef_ref[pl.ds(at, 8), :]

        def take(r):
            return coef[:, r : r + 1]

        local = local_filter(coef, four(first, keep_ref, recv_ref, topics, at))
        entering = jnp.zeros_like(local[0])
        ahead = jnp.zeros_like(local[0])
        for j in range(chips):
            far = far_ref[j, pl.ds(at, 8), :].astype(F32)
            entering = entering + take(WF0 + j) * far
            ahead = ahead + take(WQ0 + j) * far
        after = ahead + take(KNEXT) * (local[3] + take(PHI) * entering)
        middle = after
        for u in (3, 2):
            weight = take(S0 + u)
            middle = (1.0 - weight) * (local[u] + take(PHI0 + u) * entering) + weight * middle
        half = local[1] + take(PHI0 + 1) * entering
        own_ref[0, pl.ds(at, 8), :] = jnp.where(first, entering, half)
        own_ref[1, pl.ds(at, 8), :] = jnp.where(first, middle, after)
        other_ref[0, pl.ds(at, 8), :] = jnp.where(first, half, entering).astype(BF16)
        other_ref[1, pl.ds(at, 8), :] = jnp.where(first, after, middle).astype(BF16)
        return carry

    lax.fori_loop(0, topics // 8, block, 0, unroll=5)


def means_kernel(where_ref, coef_ref, keep_ref, send_ref, own_ref, other_ref, out_ref):
    _, topics, words = out_ref.shape
    half = words // 2
    first = where_ref[1] == 0

    def block(i, carry):
        at = pl.multiple_of(i * 8, 8)
        coef = coef_ref[pl.ds(at, 8), :]

        def take(r):
            return jnp.where(first, coef[:, r : r + 1], coef[:, r + 2 : r + 3])

        gain, weight, level = ([take(r + u) for u in range(2)] for r in (G0, S0, H0))
        sides = []
        for value_ref, edge_ref in ((keep_ref, own_ref), (send_ref, other_ref)):
            values = [value_ref[pl.ds(u * topics + at, 8), :] for u in range(2)]
            early = (1.0 - gain[0]) * edge_ref[0, pl.ds(at, 8), :].astype(F32) + gain[0] * values[0]
            late = (1.0 - gain[1]) * early + gain[1] * values[1]
            late = (1.0 - weight[1]) * late + weight[1] * edge_ref[1, pl.ds(at, 8), :].astype(F32)
            early = (1.0 - weight[0]) * early + weight[0] * late
            sides.append((early + level[0], late + level[1]))
        for u in range(2):
            out_ref[u, pl.ds(at, 8), :half] = jnp.where(first, sides[0][u], sides[1][u])
            out_ref[u, pl.ds(at, 8), half:] = jnp.where(first, sides[1][u], sides[0][u])
        return carry

    lax.fori_loop(0, topics // 8, block, 0, unroll=5)


def per_device(beta_mean, word_ids, word_counts, doc_slice, dirichlet, drift_var, obs_var):
    slice_dev, vocab_shard, topics = beta_mean.shape
    docs, width = word_ids.shape
    peers = lax.axis_size("doc")
    time_peers = lax.axis_size("tm")
    here = lax.axis_index("tm")
    chip, core = here // 2, here % 2
    chips = time_peers // 2
    shift = vocab_shard.bit_length() - 1
    slots = docs * width
    capacity = slots * 5 // (4 * peers)
    places = peers * capacity
    half = vocab_shard // 2
    rows = slice_dev * topics
    tail = topics - HEAD
    packed = capacity + tail + tail // 3
    groups = 4
    pack = 4
    where = jnp.stack([chip, core]).astype(I32)

    def local(*dims, dtype=F32):
        return pltpu.VMEM(dims, dtype)

    beta = jnp.swapaxes(beta_mean, 1, 2)
    code, doc, count = call(
        functools.partial(place_kernel, peers, capacity, shift, slice_dev),
        [local(peers, capacity)] * 3,
        doc_slice,
        where,
        word_ids,
        word_counts,
        scalars=2,
    )
    top = jnp.max(beta, axis=2)
    mass = jnp.sum(jnp.exp(beta - top[:, :, None]), axis=2)
    stats = jnp.concatenate([top.reshape(1, 1, -1), mass.reshape(1, 1, -1)], axis=2)
    outgoing = jnp.concatenate(
        [code.reshape(peers, 1, capacity), jnp.broadcast_to(stats, (peers, 1, stats.shape[2]))], axis=2
    )

    def exchange(value):
        return lax.all_to_all(value, "doc", split_axis=0, concat_axis=0, tiled=True)

    arrived = exchange(outgoing)
    (coef,) = call(
        functools.partial(coef_kernel, chips),
        [local(topics, NCOEF)],
        where,
        drift_var.reshape(1, topics),
        obs_var.reshape(1, topics),
        scalars=1,
        scratch=[local(NCOEF, 2 * HEAD)],
    )
    asked = arrived[:, 0, :capacity]
    tops = arrived[:, 0, capacity : capacity + rows]
    masses = arrived[:, 0, capacity + rows :]
    highest = jnp.max(tops, axis=0)
    log_norm = highest + jnp.log(jnp.sum(masses * jnp.exp(tops - highest), axis=0))
    log_norm = jnp.pad(log_norm, (0, 4 * HEAD - rows)).reshape(1, -1)
    flat = local(groups, places // groups)
    table, fetched = call(
        functools.partial(fetch_kernel, shift),
        [pltpu.HBM((rows, vocab_shard), BF16), pltpu.HBM((peers, packed, HEAD), BF16)],
        beta.reshape(rows, vocab_shard),
        log_norm,
        asked,
        scratch=[flat],
    )
    got = exchange(fetched)
    gamma, factors = call(
        estep_kernel,
        [shape((docs, topics), F32), shape((peers, docs + tail // 3 + 8, HEAD), BF16)],
        got,
        doc,
        count,
        word_counts,
        dirichlet.reshape(1, topics),
        scratch=[
            local(places, HEAD, dtype=BF16),
            local(tail, places),
            local(tail, places, dtype=BF16),
            local(1, places),
            local(1, places),
        ],
    )
    asked_late, factors = lax.optimization_barrier((asked, factors))
    factors = exchange(factors)
    low, block, key = call(
        functools.partial(index_kernel, shift, docs, pack),
        [local(places, 2 * HEAD, dtype=BF16), local(1, places), local(1, places)],
        asked_late,
        scratch=[flat],
    )
    factors, low, block, key = lax.optimization_barrier((factors, low, block, key))
    send, factor, table = call(
        functools.partial(send_kernel, docs, capacity),
        [local(rows, half), local(topics, places, dtype=BF16), local(rows, vocab_shard, dtype=BF16)],
        where,
        factors,
        key,
        low,
        block,
        table,
        scalars=1,
        far=1,
        scratch=[local(1, pack * capacity), pltpu.SemaphoreType.DMA(())],
    )
    swap = [(i, i ^ 1) for i in range(time_peers)]
    recv = lax.ppermute(send, "tm", swap)
    (keep,) = call(keep_kernel, [local(rows, half)], where, factor, low, block, table, scalars=1)
    (combined,) = call(
        combine_kernel, [shape((chips, topics, half), BF16)], where, coef, keep, recv, scalars=1
    )
    far = lax.all_to_all(
        combined,
        "tm",
        split_axis=0,
        concat_axis=0,
        tiled=True,
        axis_index_groups=[[2 * i + c for i in range(chips)] for c in range(2)],
    )
    own, other = call(
        edges_kernel,
        [local(slice_dev, topics, half), local(slice_dev, topics, half, dtype=BF16)],
        where,
        coef,
        keep,
        recv,
        far,
        scalars=1,
    )
    partner = lax.ppermute(other, "tm", swap)
    (means,) = call(
        means_kernel,
        [shape((slice_dev, topics, vocab_shard), F32)],
        where,
        coef,
        keep,
        send,
        own,
        partner,
        scalars=1,
    )
    return jnp.swapaxes(means, 1, 2), gamma


def solution(mesh):
    return jax.shard_map(
        per_device,
        mesh=mesh,
        in_specs=(
            P("tm", "doc", None),
            P(("tm", "doc"), None),
            P(("tm", "doc"), None),
            P(("tm", "doc")),
            P(),
            P(),
            P(),
        ),
        out_specs=(P("tm", "doc", None), P(("tm", "doc"), None)),
        check_vma=False,
    )
```

```python
import functools
import math

import jax
import jax.numpy as jnp
from jax import lax
from jax.experimental import pallas as pl
from jax.experimental.pallas import tpu as pltpu
from jax.sharding import PartitionSpec as P

E_ITERS = 4
PSEUDO = 0.1
PRIOR_VAR = 1.0
LOG_PSEUDO = math.log(PSEUDO)
F32, BF16, I32 = jnp.float32, jnp.bfloat16, jnp.int32
NT = (((1,), (1,)), ((), ()))
TN = (((0,), (0,)), ((), ()))
SMEM = pl.BlockSpec(memory_space=pltpu.SMEM)


def iota(shape, axis):
    return lax.broadcasted_iota(I32, shape, axis)


def hot(true):
    return true.astype(F32).astype(BF16)


def mm(a, b):
    return jnp.dot(a, b, preferred_element_type=F32)


def mmg(a, b, dims):
    return lax.dot_general(a, b, dims, preferred_element_type=F32)


VMEM = pl.BlockSpec(memory_space=pltpu.VMEM)


def shape(dims, dtype):
    return jax.ShapeDtypeStruct(dims, dtype)


def call(kernel, outs, *args, scalars=0, far=0, scratch=()):
    near = len(args) - far
    args = (
        args[:scalars]
        + tuple(pltpu.with_memory_space_constraint(a, pltpu.VMEM) for a in args[scalars:near])
        + tuple(pltpu.with_memory_space_constraint(a, pltpu.HBM) for a in args[near:])
    )
    return pl.pallas_call(
        kernel,
        out_shape=outs,
        in_specs=[SMEM] * scalars + [VMEM] * (near - scalars) + [pl.BlockSpec(memory_space=pltpu.HBM)] * far,
        out_specs=[VMEM if getattr(o, "memory_space", None) == pltpu.VMEM else pl.BlockSpec() for o in outs],
        scratch_shapes=scratch,
        compiler_params=pltpu.CompilerParams(vmem_limit_bytes=36 << 20),
    )(*args)


HEAD = 128


def open_kernel(
    peers,
    capacity,
    shift,
    per,
    where_ref,
    slice_hbm,
    ids_hbm,
    counts_hbm,
    beta_hbm,
    beta_ref,
    out_ref,
    doc_ref,
    count_ref,
    slice_ref,
    ids_ref,
    counts_ref,
    small_sems,
    sems,
):
    small = []
    for k, (source, target) in enumerate(((ids_hbm, ids_ref), (counts_hbm, counts_ref), (slice_hbm, slice_ref))):
        small.append(pltpu.make_async_copy(source, target, small_sems.at[k]))
        small[k].start()
    size = beta_ref.shape[0] // sems.shape[0]
    loads = []
    for c in range(sems.shape[0]):
        at = pl.ds(c * size, size)
        loads.append(pltpu.make_async_copy(beta_hbm.at[at], beta_ref.at[at], sems.at[c]))
        loads[c].start()
    for load in small:
        load.wait()
    docs, width = ids_ref.shape
    ids = ids_ref[...]
    owner = lax.shift_right_logical(ids, shift)
    word = ids & ((1 << shift) - 1)
    low = (word & 255).astype(F32)
    high = (lax.shift_right_logical(word, 8) + 1).astype(F32)
    counts = counts_ref[...].astype(F32)
    base = (where_ref[0] * 2 + where_ref[1]) * per
    before = (iota((width, width), 0) < iota((width, width), 1)).astype(F32).astype(BF16)
    owners = iota((peers, width), 0)
    ranks = iota((capacity, width), 0).astype(F32)
    hot = [(owners == owner[d : d + 1, :]).astype(F32) for d in range(docs)]
    inside = mm(jnp.concatenate(hot, axis=0).astype(BF16), before)
    start = jnp.zeros((peers, 1), F32)
    left, right = [], []
    for d in range(docs):
        mine = hot[d]
        part = ((slice_ref[d] - base) << (shift - 8)).astype(F32)
        rank = jnp.sum(mine * (inside[d * peers : (d + 1) * peers] + start), axis=0, keepdims=True)
        start = start + jnp.sum(mine, axis=1, keepdims=True)
        right.append((ranks == rank).astype(F32).astype(BF16))
        left.append(
            jnp.concatenate(
                [
                    mine * low[d : d + 1],
                    mine * (high[d : d + 1] + part),
                    mine * float(d),
                    mine * counts[d : d + 1],
                ],
                axis=0,
            ).astype(BF16)
        )
    placed = mmg(jnp.concatenate(left, axis=1), jnp.concatenate(right, axis=1), NT)
    low_p, high_p, doc_p, count_p = (placed[i * peers : (i + 1) * peers] for i in range(4))
    code = doc_p * 8192.0 + high_p * 256.0 + low_p
    doc_ref[...] = jnp.where(high_p > 0.5, doc_p, -1.0)
    count_ref[...] = count_p
    both = []
    left_side = iota((size, HEAD), 1) < HEAD // 2
    for c, load in enumerate(loads):
        load.wait()
        rows = beta_ref[c * size : (c + 1) * size, :]
        top = jnp.max(rows, axis=1, keepdims=True)
        mass = jnp.sum(jnp.exp(rows - top), axis=1, keepdims=True)
        both.append(jnp.where(left_side, top, mass))
    full = beta_ref.shape[0] // HEAD
    last = beta_ref.shape[0] - full * HEAD
    both.append(jnp.zeros((HEAD - last, HEAD), F32))
    both = jnp.transpose(jnp.concatenate(both, axis=0))
    both = [both[0:1], both[HEAD // 2 : HEAD // 2 + 1]]
    common = jnp.concatenate([b[:, k * HEAD : (k + 1) * HEAD] for b in both for k in range(full)], axis=0)
    rest = [b[:, full * HEAD : full * HEAD + last] for b in both]
    rest.append(jnp.zeros((1, 2 * HEAD - capacity - 2 * last), F32))
    rest = jnp.concatenate(rest, axis=1)
    for s in range(peers):
        second = jnp.concatenate([code[s : s + 1, HEAD:], rest], axis=1)
        out_ref[s] = jnp.concatenate([code[s : s + 1, :HEAD], second, common], axis=0)


def at_of(code):
    return (code & 8191) - 256


def word_of(code, shift):
    return at_of(code) & ((1 << shift) - 1)


def part_of(code, shift):
    return lax.shift_right_logical(at_of(code), shift) & 1


def flatten(flat_ref, rows_ref, group):
    capacity = rows_ref.shape[1]
    for s in range(rows_ref.shape[0]):
        g, i = divmod(s, group)
        flat_ref[g : g + 1, i * capacity : (i + 1) * capacity] = rows_ref[s : s + 1, :]


def flatten_codes(flat_ref, message_ref, capacity):
    groups = flat_ref.shape[0]
    group = message_ref.shape[0] // groups
    for s in range(message_ref.shape[0]):
        g, i = divmod(s, group)
        at = i * capacity
        flat_ref[g : g + 1, at : at + HEAD] = message_ref[s, 0:1, :]
        flat_ref[g : g + 1, at + HEAD : at + capacity] = message_ref[s, 1:2, : capacity - HEAD]


def log_norm_of(message_ref, rows, spare):
    full = rows // HEAD
    last = rows - full * HEAD

    def merge(top, mass):
        highest = jnp.max(top, axis=0)
        return highest + jnp.log(jnp.sum(mass * jnp.exp(top - highest[None]), axis=0))

    most = merge(message_ref[:, 2 : 2 + full, :], message_ref[:, 2 + full : 2 + 2 * full, :])
    second = message_ref[:, 1, :]
    end = merge(second[:, spare : spare + last], second[:, spare + last : spare + 2 * last])[None]
    end = jnp.concatenate([end, jnp.zeros((1, HEAD - last), F32)], axis=1)
    turned = jnp.transpose(jnp.concatenate([most, end, jnp.zeros((8 - full - 1, HEAD), F32)], axis=0))
    return jnp.concatenate([turned[:, k : k + 1] for k in range(full)] + [turned[:last, full : full + 1]], axis=0)


def tiles(count, grid, low, high):
    return [hot(grid == jnp.where(high == float(h), low, -1.0)) for h in range(count)]


def columns(source, code, shift):
    rows, words = source.shape[0] // 2, source.shape[1]
    chunk = 256
    grid = iota((256, chunk), 0).astype(F32)
    out = []
    for c in range(code.shape[1] // chunk):
        mine = code[:, c * chunk : (c + 1) * chunk]
        word = word_of(mine, shift)
        low, high = (word & 255).astype(F32), lax.shift_right_logical(word, 8).astype(F32)
        both = mm(source[...], jnp.concatenate(tiles(words // 256, grid, low, high), axis=0))
        out.append(jnp.where(part_of(mine, shift) == 0, both[:rows], both[rows:]))
    return jnp.concatenate(out, axis=1)


def fetch_kernel(shift, capacity, beta_ref, message_ref, table_ref, out_ref, flat_ref):
    rows, words = beta_ref.shape
    topics = rows // 2
    tail = topics - HEAD
    peers = message_ref.shape[0]
    groups = flat_ref.shape[0]
    group = peers // groups
    norm = log_norm_of(message_ref, rows, capacity - HEAD)
    step = 40
    for r in range(0, rows, step):
        table_ref[r : r + step, :] = jnp.exp(beta_ref[r : r + step, :] - norm[r : r + step]).astype(BF16)
    flatten_codes(flat_ref, message_ref, capacity)
    third = tail // 3
    spare = capacity - HEAD

    def one(g, carry):
        got = columns(table_ref, flat_ref[pl.ds(g, 1), :].astype(I32), shift)
        wide = jnp.transpose(got[:HEAD]).astype(BF16)
        for i in range(group):
            mine = got[HEAD:, i * capacity : (i + 1) * capacity]
            rest = [mine[b * third : (b + 1) * third, HEAD:] for b in range(3)]
            rest.append(jnp.zeros((third, HEAD - 3 * spare), F32))
            out_ref[g * group + i, 0:capacity, :] = wide[i * capacity : (i + 1) * capacity]
            out_ref[g * group + i, capacity : capacity + tail, :] = mine[:, :HEAD].astype(BF16)
            out_ref[g * group + i, capacity + tail :, :] = jnp.concatenate(rest, axis=1).astype(BF16)
        return carry

    lax.fori_loop(0, groups, one, 0)


def index_kernel(shift, docs, pack, capacity, message_ref, low_ref, block_ref, key_ref, flat_ref):
    groups, places = flat_ref.shape
    group = places // capacity
    flatten_codes(flat_ref, message_ref, capacity)
    lane = iota((1, places), 1)
    chunk = low_ref.shape[1]
    grid = iota((places, chunk), 1).astype(F32)
    for g in range(groups):
        code = flat_ref[g : g + 1, :].astype(I32)
        key = jnp.where(code == 0, -1, lax.shift_right_logical(code, 13))
        for s in range(1, group):
            more = docs if s % pack else (1 - pack) * docs
            key = key + jnp.where(lane >= s * capacity, jnp.where(code == 0, 0, more), 0)
        at = at_of(code) & ((2 << shift) - 1)
        low = (at & (chunk - 1)).astype(F32)
        key_ref[:, g * places : (g + 1) * places] = key.astype(F32)
        block_ref[:, g * places : (g + 1) * places] = lax.shift_right_logical(at, chunk.bit_length() - 1).astype(F32)
        column = jnp.transpose(jnp.broadcast_to(low, (8, places)))[:, 0:1]
        low_ref[g * places : (g + 1) * places, :] = hot(grid == column)


def digamma(value):
    correction = jnp.zeros_like(value)
    for j in range(6):
        correction = correction + 1.0 / (value + float(j))
    shifted = value + 6.0
    inverse = 1.0 / shifted
    square = inverse * inverse
    series = square * (1.0 / 12.0 - square * (1.0 / 120.0 - square * (1.0 / 252.0)))
    return jnp.log(shifted) - 0.5 * inverse - series - correction


def split(value):
    high = value.astype(BF16)
    return high, (value - high.astype(F32)).astype(BF16)


def estep_kernel(
    got_ref, doc_rows, count_rows, counts_ref, dirichlet_ref, gamma_ref, out_ref, head_ref, wide_ref, tail_ref, doc_ref, count_ref
):
    docs = counts_ref.shape[0]
    topics = dirichlet_ref.shape[1]
    tail = topics - HEAD
    third = tail // 3
    peers, capacity = doc_rows.shape
    spare = capacity - HEAD
    flatten(doc_ref, doc_rows, peers)
    flatten(count_ref, count_rows, peers)
    for s in range(peers):
        at = s * capacity
        head_ref[at : at + capacity, :] = got_ref[s, :capacity, :]
        wide_ref[:, at : at + HEAD] = got_ref[s, capacity : capacity + tail, :].astype(F32)
        left = got_ref[s, capacity + tail :, :].astype(F32)
        for b in range(3):
            wide_ref[b * third : (b + 1) * third, at + HEAD : at + capacity] = left[:, b * spare : (b + 1) * spare]
    tail_ref[...] = wide_ref[...].astype(BF16)
    dirichlet = dirichlet_ref[...]
    total = jnp.sum(counts_ref[...].astype(F32), axis=1, keepdims=True)
    gamma = dirichlet + total / float(topics)
    doc = doc_ref[...]
    mask = iota((docs, doc.shape[1]), 0) == doc.astype(I32)
    for step in range(E_ITERS):
        theta = jnp.exp(digamma(gamma) - digamma(jnp.sum(gamma, axis=1, keepdims=True)))
        both = jnp.concatenate(split(theta), axis=0)
        norm = mmg(both[:, :HEAD], head_ref[...], NT) + mm(both[:, HEAD:], tail_ref[...])
        norm = norm[:docs] + norm[docs:]
        norm = jnp.sum(jnp.where(mask, norm, 0.0), axis=0, keepdims=True)
        ratio = jnp.where(doc >= 0.0, count_ref[...] / norm, 0.0)
        high, low = split(ratio)
        high, low = high.astype(F32), low.astype(F32)
        spread = jnp.concatenate([jnp.where(mask, high, 0.0), jnp.where(mask, low, 0.0)], axis=0).astype(BF16)
        part = jnp.concatenate([mm(spread, head_ref[...]), mmg(spread, tail_ref[...], NT)], axis=1)
        gamma = dirichlet + theta * (part[:docs] + part[docs:])
    gamma_ref[...] = gamma
    turned = jnp.transpose(jnp.concatenate([theta[:, HEAD:], jnp.zeros((docs, 2 * HEAD - topics), F32)], axis=1))
    turned = [turned[b * third : (b + 1) * third, :] for b in range(3)]
    turned.append(jnp.zeros((third, HEAD - 3 * docs), F32))
    common = jnp.concatenate([theta[:, :HEAD], jnp.concatenate(turned, axis=1)], axis=0).astype(BF16)
    pad = jnp.zeros((1, HEAD - spare), F32)
    blank = jnp.zeros((4, HEAD), F32)
    for s in range(peers):
        at = s * capacity
        rows = []
        for piece in (high, low):
            rows.append(piece[:, at : at + HEAD])
            rows.append(jnp.concatenate([piece[:, at + HEAD : at + capacity], pad], axis=1))
        out_ref[s, 0 : docs + third, :] = common
        out_ref[s, docs + third : docs + third + 8, :] = jnp.concatenate(rows + [blank], axis=0).astype(BF16)


def factor_of(docs, capacity, factor_in, key_ref, ratio_ref, out_ref):
    peers = factor_in.shape[0]
    topics, places = out_ref.shape[0], ratio_ref.shape[1]
    group = places // capacity
    grid = iota((group * docs, places), 0)
    third = (topics - HEAD) // 3
    spare = capacity - HEAD
    for g in range(peers // group):
        turned = []
        for i in range(group):
            block = factor_in[g * group + i, docs : docs + third + 8, :].astype(F32)
            turned.append(jnp.concatenate([block[:third, b * docs : (b + 1) * docs] for b in range(3)], axis=0))
            ratio = block[third : third + 2] + block[third + 2 : third + 4]
            ratio_ref[0:1, i * capacity : i * capacity + HEAD] = ratio[0:1]
            ratio_ref[0:1, i * capacity + HEAD : (i + 1) * capacity] = ratio[1:2, :spare]
        at = slice(g * places, (g + 1) * places)
        mask = hot(grid == key_ref[:, at].astype(I32))
        top = factor_in[g * group : (g + 1) * group, :docs, :].reshape(group * docs, HEAD)
        bottom = jnp.concatenate(turned, axis=1).astype(BF16)
        ratio = ratio_ref[...]
        out_ref[:HEAD, at] = (mmg(top, mask, TN) * ratio).astype(BF16)
        out_ref[HEAD:, at] = (mm(bottom, mask) * ratio).astype(BF16)


def half_stats(half, factor_ref, low_ref, block_ref, table_ref, out_ref):
    topics = factor_ref.shape[0]
    parts = table_ref.shape[0] // topics
    chunk = low_ref.shape[1]
    blocks = table_ref.shape[1] // chunk
    block = block_ref[...]
    for t in range(parts):
        for q in range(blocks // 2):
            h = half * (blocks // 2) + q
            here = jnp.where(block == (t * blocks + h).astype(F32), 1.0, 0.0).astype(BF16)
            total = mm(factor_ref[...] * here, low_ref[...])
            words = pl.ds(pl.multiple_of(h * chunk, chunk), chunk)
            table = table_ref[t * topics : (t + 1) * topics, words].astype(F32)
            out_ref[t * topics : (t + 1) * topics, q * chunk : (q + 1) * chunk] = jnp.log(
                1.0 + (1.0 / PSEUDO) * (table * total)
            )


def send_kernel(
    docs,
    capacity,
    where_ref,
    factor_in,
    key_ref,
    low_ref,
    block_ref,
    table_hbm,
    out_ref,
    factor_ref,
    table_ref,
    ratio_ref,
    sem,
):
    load = pltpu.make_async_copy(table_hbm, table_ref, sem)
    load.start()
    factor_of(docs, capacity, factor_in, key_ref, ratio_ref, factor_ref)
    load.wait()
    half_stats(1 - where_ref[1], factor_ref, low_ref, block_ref, table_ref, out_ref)


def keep_kernel(where_ref, factor_ref, low_ref, block_ref, table_ref, out_ref):
    half_stats(where_ref[1], factor_ref, low_ref, block_ref, table_ref, out_ref)


G0, S0, H0, B0, PHI0, QK, KNEXT, PHI, WF0, WQ0, NCOEF = 0, 4, 8, 12, 16, 20, 21, 22, 23, 27, 32


def coef_kernel(chips, chip_ref, drift_ref, obs_ref, out_ref, rows_ref):
    per = 4
    length = chips * per
    drift, obs = drift_ref[...], obs_ref[...]
    one, zero = jnp.ones_like(drift), jnp.zeros_like(drift)
    var = one * PRIOR_VAR
    gain, smooth = [], []
    for t in range(length):
        pred = var + drift
        now = pred / (pred + obs)
        var = (1.0 - now) * pred
        gain.append(now)
        smooth.append(var / (var + drift) if t < length - 1 else zero)
    level, forward = zero, []
    for t in range(length):
        level = (1.0 - gain[t]) * level + gain[t]
        forward.append(level)
    ones_smoothed = [None] * length
    level = zero
    for t in reversed(range(length)):
        level = (1.0 - smooth[t]) * forward[t] + smooth[t] * level
        ones_smoothed[t] = level
    beta, phi, sigma, kappa = [], [], [], []
    for c in range(chips):
        run, back, k = one, one, zero
        for t in range(c * per, (c + 1) * per):
            run = run * (1.0 - gain[t])
            phi.append(run)
            beta.append(back * (1.0 - smooth[t]))
            k = k + beta[t] * run
            back = back * smooth[t]
        sigma.append(back)
        kappa.append(k)
    total = [phi[c * per + per - 1] for c in range(chips)]
    lead = [zero] * (chips + 1)
    for c in reversed(range(chips)):
        lead[c] = kappa[c] + sigma[c] * lead[c + 1] * total[c]
    chip = chip_ref[0]
    for c in range(chips):
        rows = [None] * NCOEF
        for u in range(per):
            t = c * per + u
            rows[G0 + u], rows[S0 + u], rows[H0 + u] = gain[t], smooth[t], ones_smoothed[t] * LOG_PSEUDO
            rows[B0 + u], rows[PHI0 + u] = beta[t], phi[t]
        rows[QK], rows[KNEXT], rows[PHI] = sigma[c] * lead[c + 1], lead[c + 1], total[c]
        for j in range(chips):
            behind, ahead = zero, zero
            if j < c:
                behind = one
                for m in range(j + 1, c):
                    behind = behind * total[m]
            if j > c:
                ahead = one
                for m in range(c + 1, j):
                    ahead = ahead * sigma[m]
            rows[WF0 + j], rows[WQ0 + j] = behind, ahead

        @pl.when(chip == c)
        def _():
            for r in range(NCOEF):
                rows_ref[r : r + 1, : drift.shape[1]] = zero if rows[r] is None else rows[r]

    out_ref[...] = jnp.transpose(rows_ref[...])[: out_ref.shape[0]]


def local_filter(coef, values):
    out, level = [], None
    for u in range(4):
        gain = coef[:, G0 + u : G0 + u + 1]
        level = gain * values[u] if level is None else (1.0 - gain) * level + gain * values[u]
        out.append(level)
    return out


def four(first, keep_ref, recv_ref, topics, at):
    own = [keep_ref[pl.ds(u * topics + at, 8), :] for u in range(2)]
    other = [recv_ref[pl.ds(u * topics + at, 8), :] for u in range(2)]
    return [jnp.where(first, own[u], other[u]) for u in range(2)] + [
        jnp.where(first, other[u], own[u]) for u in range(2)
    ]


def combine_kernel(where_ref, coef_ref, keep_ref, recv_ref, out_ref):
    chips, topics, _ = out_ref.shape
    first, chip = where_ref[1] == 0, where_ref[0]

    def block(i, carry):
        at = pl.multiple_of(i * 8, 8)
        coef = coef_ref[pl.ds(at, 8), :]
        local = local_filter(coef, four(first, keep_ref, recv_ref, topics, at))
        back = coef[:, QK : QK + 1] * local[3]
        for u in range(4):
            back = back + coef[:, B0 + u : B0 + u + 1] * local[u]
        for j in range(chips):
            out_ref[j, pl.ds(at, 8), :] = jnp.where(j > chip, local[3], back).astype(BF16)
        return carry

    lax.fori_loop(0, topics // 8, block, 0, unroll=5)


def edges_kernel(where_ref, coef_ref, keep_ref, recv_ref, far_ref, own_ref, other_ref):
    chips, topics, _ = far_ref.shape
    first = where_ref[1] == 0

    def block(i, carry):
        at = pl.multiple_of(i * 8, 8)
        coef = coef_ref[pl.ds(at, 8), :]

        def take(r):
            return coef[:, r : r + 1]

        local = local_filter(coef, four(first, keep_ref, recv_ref, topics, at))
        entering = jnp.zeros_like(local[0])
        ahead = jnp.zeros_like(local[0])
        for j in range(chips):
            far = far_ref[j, pl.ds(at, 8), :].astype(F32)
            entering = entering + take(WF0 + j) * far
            ahead = ahead + take(WQ0 + j) * far
        after = ahead + take(KNEXT) * (local[3] + take(PHI) * entering)
        middle = after
        for u in (3, 2):
            weight = take(S0 + u)
            middle = (1.0 - weight) * (local[u] + take(PHI0 + u) * entering) + weight * middle
        half = local[1] + take(PHI0 + 1) * entering
        own_ref[0, pl.ds(at, 8), :] = jnp.where(first, entering, half)
        own_ref[1, pl.ds(at, 8), :] = jnp.where(first, middle, after)
        other_ref[0, pl.ds(at, 8), :] = jnp.where(first, half, entering).astype(BF16)
        other_ref[1, pl.ds(at, 8), :] = jnp.where(first, after, middle).astype(BF16)
        return carry

    lax.fori_loop(0, topics // 8, block, 0, unroll=5)


def means_kernel(where_ref, coef_ref, keep_ref, send_ref, own_ref, other_ref, out_ref):
    _, topics, words = out_ref.shape
    half = words // 2
    first = where_ref[1] == 0

    def block(i, carry):
        at = pl.multiple_of(i * 8, 8)
        coef = coef_ref[pl.ds(at, 8), :]

        def take(r):
            return jnp.where(first, coef[:, r : r + 1], coef[:, r + 2 : r + 3])

        gain, weight, level = ([take(r + u) for u in range(2)] for r in (G0, S0, H0))
        sides = []
        for value_ref, edge_ref in ((keep_ref, own_ref), (send_ref, other_ref)):
            values = [value_ref[pl.ds(u * topics + at, 8), :] for u in range(2)]
            early = (1.0 - gain[0]) * edge_ref[0, pl.ds(at, 8), :].astype(F32) + gain[0] * values[0]
            late = (1.0 - gain[1]) * early + gain[1] * values[1]
            late = (1.0 - weight[1]) * late + weight[1] * edge_ref[1, pl.ds(at, 8), :].astype(F32)
            early = (1.0 - weight[0]) * early + weight[0] * late
            sides.append((early + level[0], late + level[1]))
        for u in range(2):
            out_ref[u, pl.ds(at, 8), :half] = jnp.where(first, sides[0][u], sides[1][u])
            out_ref[u, pl.ds(at, 8), half:] = jnp.where(first, sides[1][u], sides[0][u])
        return carry

    lax.fori_loop(0, topics // 8, block, 0, unroll=5)


def per_device(beta_mean, word_ids, word_counts, doc_slice, dirichlet, drift_var, obs_var):
    slice_dev, vocab_shard, topics = beta_mean.shape
    docs, width = word_ids.shape
    peers = lax.axis_size("doc")
    time_peers = lax.axis_size("tm")
    here = lax.axis_index("tm")
    chip, core = here // 2, here % 2
    chips = time_peers // 2
    shift = vocab_shard.bit_length() - 1
    slots = docs * width
    capacity = slots * 5 // (4 * peers)
    places = peers * capacity
    half = vocab_shard // 2
    rows = slice_dev * topics
    tail = topics - HEAD
    packed = capacity + tail + tail // 3
    groups = 4
    pack = 4
    where = jnp.stack([chip, core]).astype(I32)

    def local(*dims, dtype=F32):
        return pltpu.VMEM(dims, dtype)

    beta = jnp.swapaxes(beta_mean, 1, 2)
    beta, outgoing, doc, count = call(
        functools.partial(open_kernel, peers, capacity, shift, slice_dev),
        [local(rows, vocab_shard), local(peers, 8, HEAD), local(peers, capacity), local(peers, capacity)],
        where,
        doc_slice,
        word_ids,
        word_counts,
        beta.reshape(rows, vocab_shard),
        scalars=1,
        far=4,
        scratch=[
            pltpu.SMEM((docs,), I32),
            local(docs, width, dtype=I32),
            local(docs, width, dtype=I32),
            pltpu.SemaphoreType.DMA((3,)),
            pltpu.SemaphoreType.DMA((5,)),
        ],
    )

    def exchange(value):
        return lax.all_to_all(value, "doc", split_axis=0, concat_axis=0, tiled=True)

    arrived = exchange(outgoing)
    (coef,) = call(
        functools.partial(coef_kernel, chips),
        [local(topics, NCOEF)],
        where,
        drift_var.reshape(1, topics),
        obs_var.reshape(1, topics),
        scalars=1,
        scratch=[local(NCOEF, 2 * HEAD)],
    )
    flat = local(groups, places // groups)
    table, fetched = call(
        functools.partial(fetch_kernel, shift, capacity),
        [pltpu.HBM((rows, vocab_shard), BF16), pltpu.HBM((peers, packed, HEAD), BF16)],
        beta,
        arrived,
        scratch=[flat],
    )
    got = exchange(fetched)
    gamma, factors = call(
        estep_kernel,
        [shape((docs, topics), F32), shape((peers, docs + tail // 3 + 8, HEAD), BF16)],
        got,
        doc,
        count,
        word_counts,
        dirichlet.reshape(1, topics),
        scratch=[
            local(places, HEAD, dtype=BF16),
            local(tail, places),
            local(tail, places, dtype=BF16),
            local(1, places),
            local(1, places),
        ],
    )
    arrived, factors = lax.optimization_barrier((arrived, factors))
    factors = exchange(factors)
    low, block, key = call(
        functools.partial(index_kernel, shift, docs, pack, capacity),
        [local(places, 2 * HEAD, dtype=BF16), local(1, places), local(1, places)],
        arrived,
        scratch=[flat],
    )
    factors, low, block, key = lax.optimization_barrier((factors, low, block, key))
    send, factor, table = call(
        functools.partial(send_kernel, docs, capacity),
        [local(rows, half), local(topics, places, dtype=BF16), local(rows, vocab_shard, dtype=BF16)],
        where,
        factors,
        key,
        low,
        block,
        table,
        scalars=1,
        far=1,
        scratch=[local(1, pack * capacity), pltpu.SemaphoreType.DMA(())],
    )
    swap = [(i, i ^ 1) for i in range(time_peers)]
    recv = lax.ppermute(send, "tm", swap)
    (keep,) = call(keep_kernel, [local(rows, half)], where, factor, low, block, table, scalars=1)
    (combined,) = call(
        combine_kernel, [shape((chips, topics, half), BF16)], where, coef, keep, recv, scalars=1
    )
    far = lax.all_to_all(
        combined,
        "tm",
        split_axis=0,
        concat_axis=0,
        tiled=True,
        axis_index_groups=[[2 * i + c for i in range(chips)] for c in range(2)],
    )
    own, other = call(
        edges_kernel,
        [local(slice_dev, topics, half), local(slice_dev, topics, half, dtype=BF16)],
        where,
        coef,
        keep,
        recv,
        far,
        scalars=1,
    )
    partner = lax.ppermute(other, "tm", swap)
    (means,) = call(
        means_kernel,
        [shape((slice_dev, topics, vocab_shard), F32)],
        where,
        coef,
        keep,
        send,
        own,
        partner,
        scalars=1,
    )
    return jnp.swapaxes(means, 1, 2), gamma


def solution(mesh):
    return jax.shard_map(
        per_device,
        mesh=mesh,
        in_specs=(
            P("tm", "doc", None),
            P(("tm", "doc"), None),
            P(("tm", "doc"), None),
            P(("tm", "doc")),
            P(),
            P(),
            P(),
        ),
        out_specs=(P("tm", "doc", None), P(("tm", "doc"), None)),
        check_vma=False,
    )
```
